128 devices in a mesh: blk: 16 (over z, y), slab: 2 (over x_hi), micro: 4 (over x_lo, core).
Axes of the slice: x: 4 (x_hi: 2, x_lo: 2; x = x_hi * 2 + x_lo), y: 4, z: 4, core: 2. Of those that a mesh axis runs over, the one named last changes fastest.
Arguments:
- displacement: float32 [128, 128, 256], P('blk', 'micro', 'slab'), may hold values from -6 to 6
- load_field: float32 [128, 128, 256], P('blk', 'micro', 'slab'), may hold values from -6 to 6
- foundation: float32 [128, 128, 256], P('blk', 'micro', 'slab'), may hold values from 0.2 to 2
- plastic_flags: int32 [128, 128, 256], P('blk', 'micro', 'slab'), may hold values 0 or 1
- point_slot: int32 [128, 128, 256], P('blk', 'micro', 'slab'), may hold values from 0 to 65535, as said below
- family_in: float32 [4, 3, 256], replicated, may hold values from -5 to 5
- family_mid: bfloat16 [4, 256, 256], replicated, may hold values from -0.375 to 0.375
- family_out: bfloat16 [4, 3, 256], replicated, may hold values from -0.375 to 0.375
- family_tan: float32 [4, 256], replicated, may hold values from 0.002 to 0.02
Outputs:
- updated_field: float32 [128, 128, 256], P('blk', 'micro', 'slab')
- solver_residual: float32 [128, 128, 256], P('blk', 'micro', 'slab')
The draws below stay inside these ranges and needn't reach their ends.
Inputs may be any that keep to these rules, and one draw needn't show every extreme that they name: `point_slot`: within each device's block of 8 x 32 x 128 nodes the values are distinct; value // 16384 is the point's fibre family and value % 16384 its position among that family's points of the block in node order (last dimension fastest); in every block one family holds exactly 16384 points.
All inputs are finite; a program needn't handle non-finite values. No bound on the sum of `plastic_flags` on one device may be relied on, other than what follows from the above.
Results may differ from the reference program's by a relative error of at most 0.0024.
Values sent between devices are 32-bit elements; how exact they have to be, the bound alone decides.
A program may use at most 128 MiB of HBM per device.

```python
import math
import jax
import jax.numpy as jnp
from jax import lax

CX = 8
CY = 32
CZ = 128
MODES = 256
ITERS = 8
FAMILIES = 4
CAP = 16384
NX = 128
NY = 128
NZ = 256


def draw_point_slot(key, part):
    blocks_x = NX // CX
    blocks_y = NY // CY
    blocks_z = NZ // CZ
    block_count = blocks_x * blocks_y * blocks_z
    points_dev = CX * CY * CZ
    all_keys = jax.random.split(jax.random.fold_in(key, 17), block_count)

    def draw_block(block_key):
        key_heavy, key_order, key_other = jax.random.split(block_key, 3)
        heaviest = jax.random.randint(key_heavy, (), 0, FAMILIES)
        ordering = jax.random.permutation(key_order, points_dev)
        ranking = jnp.argsort(ordering, stable=True)
        others = (heaviest + 1 + jax.random.randint(key_other, (points_dev,), 0, FAMILIES - 1)) % FAMILIES
        family = jnp.where(ranking < CAP, heaviest, others).astype(jnp.int32)
        one_hot = (family[:, None] == jnp.arange(FAMILIES, dtype=jnp.int32)[None, :]).astype(jnp.int32)
        before = jnp.cumsum(one_hot, axis=0) - one_hot
        within = jnp.sum(before * one_hot, axis=1)
        return (family * CAP + within).astype(jnp.int32)
    slots = jax.vmap(draw_block)(all_keys)
    return slots.reshape(blocks_x, blocks_y, blocks_z, CX, CY, CZ).transpose(0, 3, 1, 4, 2, 5).reshape(NX, NY, NZ)


def plant(result, rng, least, high):
    dims = result.shape
    spot = [jax.random.randint(jax.random.fold_in(rng, axis), (), 0, dims[axis]) for axis in range(len(dims))]
    result = result.at[tuple(spot)].set(least)
    longest = dims.index(max(dims))
    spot[longest] = (spot[longest] + 1) % dims[longest]
    return result.at[tuple(spot)].set(high)


def shard_levels(stream_key, shape, cuts, smallest, top_value):
    factor_of = 1.0
    for dim, parts in cuts:
        steps = jax.random.uniform(jax.random.fold_in(jax.random.fold_in(stream_key, 6), dim), (parts,), jnp.float32, smallest / len(cuts), top_value / len(cuts))
        factor_of = factor_of * jnp.repeat(jnp.exp(steps), shape[dim] // parts).reshape((-1,) + (1,) * (len(shape) - 1 - dim))
    return factor_of


def scatter_about(rng, extent, width, bound, shards=(), kind=jnp.bfloat16):
    result = width * jax.random.normal(rng, extent, jnp.float32)
    if shards:
        result = result * shard_levels(rng, extent, shards, -0.22, 0.18)
    return jnp.clip(result, -bound, bound).astype(kind)


def setup_inputs(seed: int = 0) -> dict:
    key_list = jax.random.split(jax.random.key(seed), 10)
    return {
        "displacement": scatter_about(key_list[0], (NX, NY, NZ), 1.0, 6.0, ((0, 16), (1, 4), (2, 2)), jnp.float32),
        "load_field": scatter_about(key_list[1], (NX, NY, NZ), 1.0, 6.0, ((0, 16), (1, 4), (2, 2)), jnp.float32),
        "foundation": jnp.clip(jnp.exp(math.log(2.0) - 2.3025851 * jax.random.uniform(key_list[2], (NX, NY, NZ), jnp.float32) ** shard_levels(key_list[2], (NX, NY, NZ), ((0, 16), (1, 4), (2, 2)), -0.2, 0.2)), 0.2, 2.0),
        "plastic_flags": plant((jax.random.randint(key_list[3], (NX, NY, NZ), 0, 2) < 1).astype(jnp.int32), jax.random.fold_in(key_list[3], 1), 0, 1),
        "point_slot": draw_point_slot(jax.random.fold_in(key_list[9], 71), 0),
        "family_in": scatter_about(key_list[5], (FAMILIES, 3, MODES), 1.0, 5.0, (), jnp.float32),
        "family_mid": scatter_about(key_list[6], (FAMILIES, MODES, MODES), MODES ** -0.5, 0.375),
        "family_out": scatter_about(key_list[7], (FAMILIES, 3, MODES), MODES ** -0.5, 0.375),
        "family_tan": jnp.clip(jnp.exp(jax.random.uniform(key_list[8], (FAMILIES, MODES), jnp.float32, math.log(0.002), math.log(0.02))), 0.002, 0.02),
    }


def central_diff(values, dim_index):
    if dim_index == 0:
        return (jnp.roll(values, -1, 0) - jnp.roll(values, 1, 0)) * 0.5
    widths = [(0, 0), (0, 0), (0, 0)]
    widths[dim_index] = (1, 1)
    padded = jnp.pad(values, widths)
    length = values.shape[dim_index]
    upper_side = lax.slice_in_dim(padded, 2, length + 2, axis=dim_index)
    lower_side = lax.slice_in_dim(padded, 0, length, axis=dim_index)
    return (upper_side - lower_side) * 0.5


def fibre_model(block_rows, weight_in, weight_mid, weight_out, weight_tan):
    modal = weight_in[0][:, None] * block_rows[0][None, :] + weight_in[1][:, None] * block_rows[1][None, :] + weight_in[2][:, None] * block_rows[2][None, :]
    active = jnp.where(block_rows[3][None, :] > 0.5, jnp.tanh(modal), modal).astype(jnp.bfloat16)
    hidden = jnp.dot(weight_mid, active, preferred_element_type=jnp.float32)
    bounded = jnp.tanh(hidden).astype(jnp.bfloat16)
    stress = jnp.dot(weight_out, bounded, preferred_element_type=jnp.float32)
    widened = bounded.astype(jnp.float32)
    tangent = 0.5 + jnp.dot(weight_tan, widened * widened, precision=lax.Precision.HIGHEST)
    return jnp.concatenate([stress, tangent[None, :]], axis=0)


def reference(displacement, load_field, foundation, plastic_flags, point_slot, family_in, family_mid, family_out, family_tan):
    strains = [central_diff(displacement, dim_index) for dim_index in range(3)]
    payload = jnp.stack(strains + [plastic_flags.astype(jnp.float32)], axis=0)
    blocks_x = NX // CX
    blocks_y = NY // CY
    blocks_z = NZ // CZ
    block_count = blocks_x * blocks_y * blocks_z
    points_dev = CX * CY * CZ
    blocked_rows = payload.reshape(4, blocks_x, CX, blocks_y, CY, blocks_z, CZ).transpose(1, 3, 5, 0, 2, 4, 6).reshape(block_count, 4, points_dev)
    blocked_slots = point_slot.reshape(blocks_x, CX, blocks_y, CY, blocks_z, CZ).transpose(0, 2, 4, 1, 3, 5).reshape(block_count, points_dev)

    def evaluate_block(inputs):
        block_rows, block_slots = inputs
        padded = jnp.zeros((4, FAMILIES * CAP), jnp.float32).at[:, block_slots].set(block_rows)
        results = [fibre_model(padded[:, family_index * CAP:(family_index + 1) * CAP], family_in[family_index], family_mid[family_index], family_out[family_index], family_tan[family_index]) for family_index in range(FAMILIES)]
        merged = jnp.concatenate(results, axis=1)
        return merged[:, block_slots]

    evaluated = lax.map(evaluate_block, (blocked_rows, blocked_slots))
    answers = evaluated.reshape(blocks_x, blocks_y, blocks_z, 4, CX, CY, CZ).transpose(3, 0, 4, 1, 5, 2, 6).reshape(4, NX, NY, NZ)
    tangent = answers[3]
    rhs = load_field - foundation * displacement + (central_diff(answers[0], 0) + central_diff(answers[1], 1) + central_diff(answers[2], 2))

    def stiffness(values):
        total = central_diff(tangent * central_diff(values, 0), 0) + central_diff(tangent * central_diff(values, 1), 1) + central_diff(tangent * central_diff(values, 2), 2)
        return foundation * values - total

    solution = jnp.zeros_like(rhs)
    residual = rhs
    direction = rhs
    current = jnp.sum(residual * residual)
    for iteration in range(ITERS):
        image = stiffness(direction)
        alpha = current / jnp.sum(direction * image)
        solution = solution + alpha * direction
        residual = residual - alpha * image
        following = jnp.sum(residual * residual)
        direction = residual + (following / current) * direction
        current = following
    return displacement + solution, residual
```

```python
import jax
import jax.numpy as jnp
from jax import lax
from jax.experimental import pallas as pl
from jax.experimental.pallas import tpu as pltpu
from jax.sharding import PartitionSpec as P

F32 = jnp.float32
BF16 = jnp.bfloat16
MESH = pl.DeviceIdType.MESH
FAMILIES = 4
MODES = 256
CAP_SHIFT = 14
ROWS = 16
SIGMA = 3.0
NX, NY, NZ = 8, 32, 128
TILES = NY // 8
E_DISP, E_TAN, E_SX, E_SY, E_R, E_W, E_T = 0, 1, 2, 3, 4, 5, 6
N_EX = 12
N_RED = 4
N_DOT = 13


def prepare_weights(family_in, family_mid, family_out, family_tan, w_in, w_mid, w_out):
    zero = jnp.zeros((1, MODES), F32)
    high, low, stress, tangent = [], [], [], []
    for f in range(FAMILIES):
        weight = family_in[f]
        rounded = weight.astype(BF16).astype(F32)
        high += [rounded, rounded, zero, zero]
        low += [weight - rounded, zero, zero, zero, zero, zero]
        w_mid[:, f * MODES : (f + 1) * MODES] = family_mid[f]
        tan = family_tan[f : f + 1, :]
        tan_high = tan.astype(BF16).astype(F32)
        stress += [family_out[f].astype(F32)] + [zero] * 5
        tangent += [zero] * 3 + [tan_high, tan - tan_high] + [zero] * 3
    w_in[...] = jnp.concatenate(high + low, axis=0).T.astype(BF16)
    w_out[:, :MODES] = jnp.concatenate(stress, axis=0).astype(BF16)
    w_out[:, MODES:] = jnp.concatenate(tangent, axis=0).astype(BF16)


def fibre_chunk(points, w_in, w_mid, w_out, base):
    width = ROWS * NZ
    rows = jnp.concatenate([points[pl.ds(base + 8 * i, 8), :] for i in range(ROWS)], axis=1)
    family, flag = rows[6:7, :], rows[7:8, :]
    family_8 = jnp.broadcast_to(family, (8, width))
    chosen = [family_8 == float(f) for f in range(FAMILIES)]
    strain = jnp.concatenate([jnp.where(m, rows, 0.0) for m in chosen], axis=0).astype(BF16)
    modal = jnp.dot(w_in[...], jnp.concatenate([strain, strain], axis=0), preferred_element_type=F32)
    modal = modal.reshape(MODES // 8, 8, width)
    plastic = jnp.broadcast_to(flag, (8, width)) > 0.5
    active = jnp.where(plastic[None], jnp.tanh(modal), modal).reshape(MODES, width).astype(BF16)
    active = active.reshape(MODES // 16, 16, width)
    family_16 = jnp.broadcast_to(family, (16, width))
    parts = []
    for f in range(FAMILIES):
        mask = jnp.where(family_16 == float(f), 1.0, 0.0).astype(BF16)
        parts.append((active * mask[None]).reshape(MODES, width))
    hidden = jnp.dot(w_mid[...], jnp.concatenate(parts, axis=0), preferred_element_type=F32)
    bounded = jnp.tanh(hidden).astype(BF16)
    out = jnp.dot(
        w_out[...], jnp.concatenate([bounded, bounded * bounded], axis=0), preferred_element_type=F32
    )
    picked = jnp.where(
        chosen[0], out[0:8], jnp.where(chosen[1], out[8:16], jnp.where(chosen[2], out[16:24], out[24:32]))
    )
    for i in range(ROWS):
        points[pl.ds(base + 8 * i, 8), :] = picked[:, i * NZ : (i + 1) * NZ]


def newton_kernel(
    disp_ref, load_ref, found_ref, flags_ref, slot_ref, fin_ref, fmid_ref, fout_ref, ftan_ref,
    field_out, residual_out,
    ex, zsend, zrecv, red, points, w_in, w_mid, w_out, coef, s_z,
    x_, r_, w_, z_, z2_, p_, s_, t_, u_, v_,
    send_sem, recv_sem, red_send, red_recv,
):
    blk, slab, micro = lax.axis_index("blk"), lax.axis_index("slab"), lax.axis_index("micro")
    n_blk = lax.axis_size("blk")
    up_blk, down_blk = lax.rem(blk + 1, n_blk), lax.rem(blk + n_blk - 1, n_blk)
    part_x = slab * 4 + micro
    part_y, part_z = lax.rem(blk, 4), lax.div(blk, 4)

    def peer_x(step):
        other = lax.rem(part_x + step, 8)
        return (blk, lax.div(other, 4), lax.rem(other, 4))

    def peer_y(step):
        return (part_z * 4 + lax.rem(part_y + step, 4), slab, micro)

    def peer_z(step):
        return (lax.rem(part_z + step, 4) * 4 + part_y, slab, micro)

    barrier = pltpu.get_barrier_semaphore()
    friends = [peer_x(j) for j in range(1, 8)] + [peer_y(j) for j in range(1, 4)]
    friends += [peer_z(j) for j in range(1, 4)] + [(up_blk, slab, micro), (down_blk, slab, micro)]
    for friend in friends:
        pl.semaphore_signal(barrier, inc=1, device_id=friend, device_id_type=MESH)

    lane = lax.broadcasted_iota(jnp.int32, (8, NZ), 1)
    first_slab, last_slab = slab == 0, slab == 1
    pack_id = lax.shift_right_logical(lax.rem(lane + 2 * (1 - slab), NZ), 1)
    edge_up = {n: jnp.logical_and(lane < n, first_slab) for n in (1, 2)}
    edge_down = {n: jnp.logical_and(lane >= NZ - n, last_slab) for n in (1, 2)}

    def keep(condition):
        return jnp.where(condition, 0.0, 1.0).astype(F32)

    keep_up_1 = keep(jnp.logical_and(lane == NZ - 1, last_slab))[None]
    keep_down_1 = keep(jnp.logical_and(lane == 0, first_slab))[None]
    keep_up_2 = keep(jnp.logical_and(lane >= NZ - 2, last_slab))[None]
    keep_down_2 = keep(jnp.logical_and(lane < 2, first_slab))[None]

    @pl.when(micro == 0)
    def _():
        for e in range(N_EX):
            ex[e, :, 0:8, :] = jnp.zeros((NX + 4, 8, NZ), F32)

    @pl.when(micro == 3)
    def _():
        for e in range(N_EX):
            ex[e, :, NY + 8 : NY + 16, :] = jnp.zeros((NX + 4, 8, NZ), F32)

    def copy(source, target, e, k, device):
        return pltpu.make_async_remote_copy(
            src_ref=source, dst_ref=target, send_sem=send_sem.at[e, k], recv_sem=recv_sem.at[e, k],
            device_id=device, device_id_type=MESH,
        )

    def copies_x(e, depth):
        up = copy(
            ex.at[e, pl.ds(NX + 2 - depth, depth), pl.ds(8, NY), :],
            ex.at[e, pl.ds(2 - depth, depth), pl.ds(8, NY), :], e, 0, (up_blk, slab, micro),
        )
        down = copy(
            ex.at[e, pl.ds(2, depth), pl.ds(8, NY), :],
            ex.at[e, pl.ds(NX + 2, depth), pl.ds(8, NY), :], e, 1, (down_blk, slab, micro),
        )
        return up, down

    def copies_y(e):
        up = copy(
            ex.at[e, pl.ds(2, NX), pl.ds(NY, 8), :], ex.at[e, pl.ds(2, NX), pl.ds(0, 8), :],
            e, 2, (blk, slab, lax.rem(micro + 1, 4)),
        )
        down = copy(
            ex.at[e, pl.ds(2, NX), pl.ds(8, 8), :], ex.at[e, pl.ds(2, NX), pl.ds(NY + 8, 8), :],
            e, 3, (blk, slab, lax.rem(micro + 3, 4)),
        )
        return up, down

    def copy_z(e):
        return copy(zsend.at[e], zrecv.at[e], e, 4, (blk, 1 - slab, micro))

    def start(e, depth, x=True, y=True, z=True):
        if x:
            for c in copies_x(e, depth):
                c.start()
        if z:
            copy_z(e).start()
        if y:
            up, down = copies_y(e)

            @pl.when(micro < 3)
            def _():
                up.start()

            @pl.when(micro > 0)
            def _():
                down.start()

    def finish(e, depth, x=True, y=True, z=True):
        if x:
            for c in copies_x(e, depth):
                c.wait_recv()
        if z:
            copy_z(e).wait_recv()
        if y:
            up, down = copies_y(e)

            @pl.when(micro > 0)
            def _():
                up.wait_recv()

            @pl.when(micro < 3)
            def _():
                down.wait_recv()

    def drain(e, depth, x=True, y=True, z=True):
        if x:
            for c in copies_x(e, depth):
                c.wait_send()
        if z:
            copy_z(e).wait_send()
        if y:
            up, down = copies_y(e)

            @pl.when(micro < 3)
            def _():
                up.wait_send()

            @pl.when(micro > 0)
            def _():
                down.wait_send()

    def pack_plane(packed, plane, i):
        for q in range(TILES):
            n = i * TILES + q
            tile = plane[8 * q : 8 * q + 8]
            packed = jnp.where(pack_id == n, pltpu.roll(tile, 2 * n, 1) if n else tile, packed)
        return packed

    def shifted_z(plane, message, i, step):
        tiles_up, tiles_down = [], []
        for q in range(TILES):
            n = i * TILES + q
            tile = plane[8 * q : 8 * q + 8]
            halo = pltpu.roll(message, NZ - 2 * n, 1) if n else message
            tiles_up.append(pltpu.roll(jnp.where(edge_up[step], halo, tile), NZ - step, 1))
            tiles_down.append(pltpu.roll(jnp.where(edge_down[step], halo, tile), step, 1))
        return jnp.concatenate(tiles_up, axis=0), jnp.concatenate(tiles_down, axis=0)

    def masked(plane, mask):
        return (plane.reshape(TILES, 8, NZ) * mask).reshape(NY, NZ)

    inner = pl.ds(8, NY)

    def put(e, i, plane):
        ex[e, 2 + i, inner, :] = plane

    def operator(e, write):
        message = zrecv[e]
        for i in range(NX):
            value = ex[e, 2 + i, inner, :]
            z_up, z_down = shifted_z(value, message, i, 2)
            total = coef[0, i] * value
            total -= coef[1, i] * ex[e, 4 + i, inner, :] + coef[2, i] * ex[e, i, inner, :]
            total -= coef[3, i] * ex[e, 2 + i, 10 : 10 + NY, :] + coef[4, i] * ex[e, 2 + i, 6 : 6 + NY, :]
            total -= coef[5, i] * z_up + coef[6, i] * z_down
            write(i, total)

    def red_copy(k, stage, step, peer, mine):
        n = stage * 8 + step
        return pltpu.make_async_remote_copy(
            src_ref=red.at[k, stage, mine], dst_ref=red.at[k, stage, mine],
            send_sem=red_send.at[k, n], recv_sem=red_recv.at[k, n], device_id=peer, device_id_type=MESH,
        )

    stages = ((peer_x, part_x, 8), (peer_y, part_y, 4), (peer_z, part_z, 4))

    def red_start(k, stage, rows):
        peer, mine, count = stages[stage]
        red[k, stage, mine] = rows
        for step in range(1, count):
            red_copy(k, stage, step, peer(step), mine).start()

    def red_finish(k, stage):
        peer, mine, count = stages[stage]
        for step in range(1, count):
            red_copy(k, stage, step, peer(step), mine).wait_recv()
        total = red[k, stage, 0]
        for j in range(1, count):
            total = total + red[k, stage, j]
        return total

    def red_drain(k):
        for stage, (peer, mine, count) in enumerate(stages):
            for step in range(1, count):
                red_copy(k, stage, step, peer(step), mine).wait_send()

    def partial_dots():
        sums = [None] * N_DOT
        for i in range(NX):
            r, w, p, s, t = r_[i], w_[i], p_[i], s_[i], t_[i]
            kp = s + SIGMA * p
            kr = w + SIGMA * r
            kkp = (t + SIGMA * s) + SIGMA * kp
            terms = (
                r * r, r * kp, r * kr, r * kkp, kp * kp, kp * kr, kp * kkp,
                kr * kr, kr * kkp, kkp * kkp, p * kp, p * kr, p * kkp,
            )
            for j, term in enumerate(terms):
                folded = term.reshape(TILES, 8, NZ).sum(axis=0)
                sums[j] = folded if i == 0 else sums[j] + folded
        rows = [jnp.sum(a, axis=0, keepdims=True) for a in sums]
        return jnp.concatenate(rows + [jnp.zeros((16 - N_DOT, NZ), F32)], axis=0)

    def scalars(rows):
        d = jnp.sum(rows, axis=1, keepdims=True)
        g = [d[j : j + 1, :] for j in range(N_DOT)]
        rr, rs, rw, rt, ss, sw, st, ww, wt, tt, ps, pw, pt = g
        alpha = rr / ps
        rr_1 = rr - 2.0 * alpha * rs + alpha * alpha * ss
        beta_1 = rr_1 / rr
        r_q = rw - alpha * rt + beta_1 * rs
        s_q = sw - alpha * st + beta_1 * ss
        p_q = pw - alpha * pt + beta_1 * ps
        alpha_1 = rr_1 / (r_q - alpha * s_q + beta_1 * p_q)
        w_q = ww - alpha * wt + beta_1 * sw
        t_q = wt - alpha * tt + beta_1 * st
        q_q = w_q - alpha * t_q + beta_1 * s_q
        rr_2 = rr_1 - 2.0 * alpha_1 * (r_q - alpha * s_q) + alpha_1 * alpha_1 * q_q
        beta_2 = rr_2 / rr_1
        return [jnp.broadcast_to(a, (NY, NZ)) for a in (alpha, beta_1, alpha_1, beta_2)]

    packed = jnp.zeros((8, NZ), F32)
    for i in range(NX):
        plane = disp_ref[i]
        put(E_DISP, i, plane)
        packed = pack_plane(packed, plane, i)
    zsend[E_DISP] = packed
    pl.semaphore_wait(barrier, len(friends))
    start(E_DISP, 1)
    prepare_weights(fin_ref, fmid_ref, fout_ref, ftan_ref, w_in, w_mid, w_out)
    finish(E_DISP, 1)
    message = zrecv[E_DISP]
    for i in range(NX):
        value = ex[E_DISP, 2 + i, inner, :]
        z_up, z_down = shifted_z(value, message, i, 1)
        strains = (
            (ex[E_DISP, 3 + i, inner, :] - ex[E_DISP, 1 + i, inner, :]) * 0.5,
            (ex[E_DISP, 2 + i, 9 : 9 + NY, :] - ex[E_DISP, 2 + i, 7 : 7 + NY, :]) * 0.5,
            (masked(z_up, keep_up_1) - masked(z_down, keep_down_1)) * 0.5,
        )
        rounded = [s.astype(BF16).astype(F32) for s in strains]
        family = lax.shift_right_logical(slot_ref[i], CAP_SHIFT).astype(F32)
        rows = rounded + [s - h for s, h in zip(strains, rounded)] + [family, flags_ref[i].astype(F32)]
        for k, row in enumerate(rows):
            points[pl.ds(i * NY * 8 + k, NY, stride=8), :] = row

    def chunk(j, carry):
        fibre_chunk(points, w_in, w_mid, w_out, pl.multiple_of(j * (8 * ROWS), 8 * ROWS))
        return carry

    lax.fori_loop(0, NX * NY // ROWS, chunk, 0)

    packed_t = packed_s = jnp.zeros((8, NZ), F32)
    for i in range(NX):
        sx, sy, sz, tan_high, tan_low = [points[pl.ds(i * NY * 8 + k, NY, stride=8), :] for k in range(5)]
        tangent = 0.5 + (tan_high + tan_low)
        put(E_SX, i, sx)
        put(E_SY, i, sy)
        put(E_TAN, i, tangent)
        s_z[i] = sz
        packed_s = pack_plane(packed_s, sz, i)
        packed_t = pack_plane(packed_t, tangent, i)
    zsend[E_SX] = packed_s
    zsend[E_TAN] = packed_t
    start(E_SX, 1, y=False)
    start(E_TAN, 1)
    start(E_SY, 1, x=False, z=False)
    finish(E_SX, 1, y=False)
    finish(E_TAN, 1)
    finish(E_SY, 1, x=False, z=False)
    message_s, message_t = zrecv[E_SX], zrecv[E_TAN]
    packed = jnp.zeros((8, NZ), F32)
    for i in range(NX):
        up, down = shifted_z(s_z[i], message_s, i, 1)
        total = (ex[E_SX, 3 + i, inner, :] - ex[E_SX, 1 + i, inner, :]) * 0.5
        total += (ex[E_SY, 2 + i, 9 : 9 + NY, :] - ex[E_SY, 2 + i, 7 : 7 + NY, :]) * 0.5
        total += (masked(up, keep_up_1) - masked(down, keep_down_1)) * 0.5
        rhs = load_ref[i] - found_ref[i] * disp_ref[i] + total
        put(E_R, i, rhs)
        packed = pack_plane(packed, rhs, i)
        r_[i] = rhs
        p_[i] = rhs
        x_[i] = jnp.zeros((NY, NZ), F32)
        u_[i] = jnp.zeros((NY, NZ), F32)
    zsend[E_R] = packed
    start(E_R, 2)
    for i in range(NX):
        up, down = shifted_z(ex[E_TAN, 2 + i, inner, :], message_t, i, 1)
        z_up, z_down = masked(up, keep_up_1) * 0.25, masked(down, keep_down_1) * 0.25
        x_up, x_down = ex[E_TAN, 3 + i, inner, :] * 0.25, ex[E_TAN, 1 + i, inner, :] * 0.25
        y_up, y_down = ex[E_TAN, 2 + i, 9 : 9 + NY, :] * 0.25, ex[E_TAN, 2 + i, 7 : 7 + NY, :] * 0.25
        coef[0, i] = found_ref[i] + ((x_up + x_down) + (y_up + y_down) + (z_up + z_down)) - SIGMA
        coef[1, i], coef[2, i] = x_up, x_down
        coef[3, i], coef[4, i] = y_up, y_down
        coef[5, i], coef[6, i] = masked(z_up, keep_up_2), masked(z_down, keep_down_2)

    class Packer:
        def __init__(self):
            self.packed = jnp.zeros((8, NZ), F32)

        def add(self, plane, i):
            self.packed = pack_plane(self.packed, plane, i)

    finish(E_R, 2)
    pack = Packer()

    def write_w(i, value):
        put(E_W, i, value)
        w_[i] = value
        s_[i] = value
        pack.add(value, i)

    operator(E_R, write_w)
    zsend[E_W] = pack.packed
    start(E_W, 2)
    finish(E_W, 2)
    pack_t = Packer()

    def write_z(i, value):
        put(E_T, i, value)
        z_[i] = value
        t_[i] = value
        pack_t.add(value, i)

    operator(E_W, write_z)
    zsend[E_T] = pack_t.packed

    def block(k, beta):
        e_t, e_u = E_T + 2 * k, E_T + 2 * k + 1
        start(e_t, 2)
        red_start(k, 0, partial_dots())
        finish(e_t, 2)
        pack_u = Packer()

        def write_u(i, value):
            put(e_u, i, value)
            z2_[i] = value - beta * u_[i]
            u_[i] = value
            pack_u.add(value, i)

        operator(e_t, write_u)
        zsend[e_u] = pack_u.packed
        start(e_u, 2)
        red_start(k, 1, red_finish(k, 0))
        red_start(k, 2, red_finish(k, 1))
        finish(e_u, 2)

        def write_v(i, value):
            v_[i] = value

        operator(e_u, write_v)
        alpha, beta_1, alpha_1, beta_2 = scalars(red_finish(k, 2))
        pack_n = Packer()
        tangents = []
        for i in range(NX):
            p, s, t, u = p_[i], s_[i], t_[i], u_[i]
            x = x_[i] + alpha * p
            r = r_[i] - alpha * (s + SIGMA * p)
            w = w_[i] - alpha * (t + SIGMA * s)
            z = z_[i] - alpha * (u + SIGMA * t)
            z2 = z2_[i] - alpha * (v_[i] + SIGMA * u)
            p = r + beta_1 * p
            s = w + beta_1 * s
            t = z + beta_1 * t
            u = z2 + beta_1 * u
            x_[i] = x + alpha_1 * p
            r = r - alpha_1 * (s + SIGMA * p)
            w = w - alpha_1 * (t + SIGMA * s)
            z = z - alpha_1 * (u + SIGMA * t)
            r_[i], w_[i], z_[i], u_[i] = r, w, z, u
            p_[i] = r + beta_2 * p
            s_[i] = w + beta_2 * s
            t = z + beta_2 * t
            t_[i] = t
            tangents.append(t)
        for i in range(NX):
            pack_n.add(tangents[i], i)

        @pl.when(k < 2)
        def _():
            for i in range(NX):
                put(e_t + 2, i, tangents[i])
            zsend[e_t + 2] = pack_n.packed

        return beta_2

    lax.fori_loop(0, 3, block, jnp.zeros((NY, NZ), F32))

    last = N_RED - 1
    red_start(last, 0, partial_dots())
    red_start(last, 1, red_finish(last, 0))
    red_start(last, 2, red_finish(last, 1))
    alpha, beta_1, alpha_1, _ = scalars(red_finish(last, 2))
    for i in range(NX):
        p, s, t = p_[i], s_[i], t_[i]
        x = x_[i] + alpha * p
        r = r_[i] - alpha * (s + SIGMA * p)
        w = w_[i] - alpha * (t + SIGMA * s)
        p = r + beta_1 * p
        s = w + beta_1 * s
        field_out[i] = disp_ref[i] + (x + alpha_1 * p)
        residual_out[i] = r - alpha_1 * (s + SIGMA * p)

    drain(E_DISP, 1)
    drain(E_SX, 1, y=False)
    drain(E_TAN, 1)
    drain(E_SY, 1, x=False, z=False)

    def drain_step(e, carry):
        drain(e, 2)
        return carry

    lax.fori_loop(E_R, N_EX, drain_step, 0)

    def drain_red(k, carry):
        red_drain(k)
        return carry

    lax.fori_loop(0, N_RED, drain_red, 0)


def body(*args):
    shape = (NX, NY, NZ)
    field = pltpu.VMEM(shape, F32)
    whole = pl.BlockSpec(memory_space=pltpu.VMEM)
    return pl.pallas_call(
        newton_kernel,
        out_shape=(jax.ShapeDtypeStruct(shape, F32), jax.ShapeDtypeStruct(shape, F32)),
        in_specs=[whole] * 9,
        out_specs=(whole, whole),
        scratch_shapes=[
            pltpu.VMEM((N_EX, NX + 4, NY + 16, NZ), F32),
            pltpu.VMEM((N_EX, 8, NZ), F32),
            pltpu.VMEM((N_EX, 8, NZ), F32),
            pltpu.VMEM((N_RED, 3, 8, 16, NZ), F32),
            pltpu.VMEM((NX * NY * 8, NZ), F32),
            pltpu.VMEM((MODES, 64), BF16),
            pltpu.VMEM((MODES, FAMILIES * MODES), BF16),
            pltpu.VMEM((32, 2 * MODES), BF16),
            pltpu.VMEM((7,) + shape, F32),
            field,
        ]
        + [field] * 10
        + [
            pltpu.SemaphoreType.DMA((N_EX, 5)),
            pltpu.SemaphoreType.DMA((N_EX, 5)),
            pltpu.SemaphoreType.DMA((N_RED, 24)),
            pltpu.SemaphoreType.DMA((N_RED, 24)),
        ],
        compiler_params=pltpu.CompilerParams(
            collective_id=0, has_side_effects=True, vmem_limit_bytes=60 * 1024 * 1024
        ),
        name="newton_step",
    )(*args)


def solution(mesh):
    placed = P("blk", "micro", "slab")
    return jax.shard_map(
        body,
        mesh=mesh,
        in_specs=(placed,) * 5 + (P(),) * 4,
        out_specs=(placed, placed),
        check_vma=False,
    )
```

```python
import jax
import jax.numpy as jnp
from jax import lax
from jax.experimental import pallas as pl
from jax.experimental.pallas import tpu as pltpu
from jax.sharding import PartitionSpec as P

F32 = jnp.float32
BF16 = jnp.bfloat16
MESH = pl.DeviceIdType.MESH
FAMILIES = 4
MODES = 256
CAP_SHIFT = 14
SIGMA = 3.0
NX, NY, NZ = 8, 32, 128
TILES = NY // 8
E_DISP, E_TAN, E_SX, E_SY, E_R, E_W, E_T = 0, 1, 2, 3, 4, 5, 6
N_EX = 12
N_RED = 4
N_IN = 12
FIX = NX * NY * 8
N_DOT = 13


def prepare_weights(family_in, family_out, family_tan, w_in, w_out):
    zero = jnp.zeros((1, MODES), F32)
    high, low, stress, tangent = [], [], [], []
    for f in range(FAMILIES):
        weight = family_in[:, f, :]
        rounded = weight.astype(BF16).astype(F32)
        high += [rounded, rounded, zero, zero]
        low += [weight - rounded, zero, zero, zero, zero, zero]
        tan = family_tan[f : f + 1, :]
        tan_high = tan.astype(BF16).astype(F32)
        stress += [family_out[:, f, :].astype(F32)] + [zero] * 5
        tangent += [zero] * 3 + [tan_high, tan - tan_high] + [zero] * 3
    w_in[...] = jnp.concatenate(high + low, axis=0).T.astype(BF16)
    w_out[:, :MODES] = jnp.concatenate(stress, axis=0).astype(BF16)
    w_out[:, MODES:] = jnp.concatenate(tangent, axis=0).astype(BF16)


def fibre_chunk(points, w_in, w_mid, w_out, bases):
    places = [base + 8 * i for base in bases for i in range(8)]
    width = len(places) * NZ
    rows = jnp.concatenate([points[pl.ds(place, 8), :] for place in places], axis=1)
    family, flag = rows[6:7, :], rows[7:8, :]
    family_8 = jnp.broadcast_to(family, (8, width))
    chosen = [family_8 == float(f) for f in range(FAMILIES)]
    strain = jnp.concatenate([jnp.where(m, rows, 0.0) for m in chosen], axis=0).astype(BF16)
    modal = jnp.dot(w_in[...], jnp.concatenate([strain, strain], axis=0), preferred_element_type=F32)
    modal = modal.reshape(MODES // 8, 8, width)
    plastic = jnp.broadcast_to(flag, (8, width)) > 0.5
    active = jnp.where(plastic[None], jnp.tanh(modal), modal).reshape(MODES, width).astype(BF16)
    active = active.reshape(MODES // 16, 16, width)
    family_16 = jnp.broadcast_to(family, (16, width))
    parts = []
    for f in range(FAMILIES):
        mask = jnp.where(family_16 == float(f), 1.0, 0.0).astype(BF16)
        parts.append((active * mask[None]).reshape(MODES, width))
    hidden = jnp.dot(w_mid[...], jnp.concatenate(parts, axis=0), preferred_element_type=F32)
    bounded = jnp.tanh(hidden).astype(BF16)
    out = jnp.dot(
        w_out[...], jnp.concatenate([bounded, bounded * bounded], axis=0), preferred_element_type=F32
    )
    picked = jnp.where(
        chosen[0], out[0:8], jnp.where(chosen[1], out[8:16], jnp.where(chosen[2], out[16:24], out[24:32]))
    )
    for i, place in enumerate(places):
        points[pl.ds(place, 8), :] = picked[:, i * NZ : (i + 1) * NZ]


def newton_kernel(
    disp_hbm, load_hbm, found_hbm, flags_hbm, slot_hbm, fin_hbm, fmid_hbm, fout_hbm, ftan_hbm,
    field_out, residual_out,
    load_ref, found_ref, flags_ref, slot_ref, fin_ref, fout_ref, ftan_ref,
    ex, zsend, zrecv, red, points, w_in, w_mid, w_out, coef, s_z,
    x_, r_, w_, z_, z2_, p_, s_, t_, u_, v_,
    send_sem, recv_sem, red_send, red_recv, in_sem,
):
    inner = pl.ds(8, NY)
    pairs = [(disp_hbm, ex.at[E_DISP, pl.ds(2, NX), inner, :]), (slot_hbm, slot_ref), (flags_hbm, flags_ref)]
    pairs += [(fin_hbm, fin_ref), (fout_hbm, fout_ref), (ftan_hbm, ftan_ref)]
    pairs += [(fmid_hbm.at[f], w_mid.at[:, pl.ds(f * MODES, MODES)]) for f in range(FAMILIES)]
    pairs += [(found_hbm, found_ref), (load_hbm, load_ref)]
    loads = [pltpu.make_async_copy(a, b, in_sem.at[j]) for j, (a, b) in enumerate(pairs)]
    for c in loads:
        c.start()
    blk, slab, micro = lax.axis_index("blk"), lax.axis_index("slab"), lax.axis_index("micro")
    n_blk = lax.axis_size("blk")
    up_blk, down_blk = lax.rem(blk + 1, n_blk), lax.rem(blk + n_blk - 1, n_blk)
    part_x = slab * 4 + micro

    def peer_x(step):
        other = lax.rem(part_x + step, 8)
        return (blk, lax.div(other, 4), lax.rem(other, 4))

    def peer_blk(step):
        return (lax.rem(blk + step, n_blk), slab, micro)

    barrier = pltpu.get_barrier_semaphore()
    friends = [peer_x(j) for j in range(1, 8)] + [peer_blk(j) for j in range(1, 16)]
    for friend in friends:
        pl.semaphore_signal(barrier, inc=1, device_id=friend, device_id_type=MESH)

    lane = lax.broadcasted_iota(jnp.int32, (8, NZ), 1)
    diagonal = lax.broadcasted_iota(jnp.int32, (16, NZ), 0) == lax.broadcasted_iota(jnp.int32, (16, NZ), 1)
    first_slab, last_slab = slab == 0, slab == 1
    pack_id = {n: lax.div(lax.rem(lane + n * (1 - slab), NZ), n) for n in (1, 2)}
    edge_own = jnp.logical_or(jnp.logical_and(lane == NZ - 1, slab == 0), jnp.logical_and(lane == 0, slab == 1))
    edge_up = {n: jnp.logical_and(lane < n, first_slab) for n in (1, 2)}
    edge_down = {n: jnp.logical_and(lane >= NZ - n, last_slab) for n in (1, 2)}

    def keep(condition):
        return jnp.where(condition, 0.0, 1.0).astype(F32)

    keep_up_1 = keep(jnp.logical_and(lane == NZ - 1, last_slab))[None]
    keep_down_1 = keep(jnp.logical_and(lane == 0, first_slab))[None]
    keep_up_2 = keep(jnp.logical_and(lane >= NZ - 2, last_slab))[None]
    keep_down_2 = keep(jnp.logical_and(lane < 2, first_slab))[None]

    @pl.when(micro == 0)
    def _():
        for e in range(N_EX):
            ex[e, :, 0:8, :] = jnp.zeros((NX + 4, 8, NZ), F32)

    @pl.when(micro == 3)
    def _():
        for e in range(N_EX):
            ex[e, :, NY + 8 : NY + 16, :] = jnp.zeros((NX + 4, 8, NZ), F32)

    def copy(source, target, e, k, device):
        return pltpu.make_async_remote_copy(
            src_ref=source, dst_ref=target, send_sem=send_sem.at[e, k], recv_sem=recv_sem.at[e, k],
            device_id=device, device_id_type=MESH,
        )

    def copies_x(e, depth):
        up = copy(
            ex.at[e, pl.ds(NX + 2 - depth, depth), pl.ds(8, NY), :],
            ex.at[e, pl.ds(2 - depth, depth), pl.ds(8, NY), :], e, 0, (up_blk, slab, micro),
        )
        down = copy(
            ex.at[e, pl.ds(2, depth), pl.ds(8, NY), :],
            ex.at[e, pl.ds(NX + 2, depth), pl.ds(8, NY), :], e, 1, (down_blk, slab, micro),
        )
        return up, down

    def copies_y(e):
        up = copy(
            ex.at[e, pl.ds(2, NX), pl.ds(NY, 8), :], ex.at[e, pl.ds(2, NX), pl.ds(0, 8), :],
            e, 2, (blk, slab, lax.rem(micro + 1, 4)),
        )
        down = copy(
            ex.at[e, pl.ds(2, NX), pl.ds(8, 8), :], ex.at[e, pl.ds(2, NX), pl.ds(NY + 8, 8), :],
            e, 3, (blk, slab, lax.rem(micro + 3, 4)),
        )
        return up, down

    def copy_z(e):
        return copy(zsend.at[e], zrecv.at[e], e, 4, (blk, 1 - slab, micro))

    def start(e, depth, x=True, y=True, z=True):
        if x:
            for c in copies_x(e, depth):
                c.start()
        if z:
            copy_z(e).start()
        if y:
            up, down = copies_y(e)

            @pl.when(micro < 3)
            def _():
                up.start()

            @pl.when(micro > 0)
            def _():
                down.start()

    def finish(e, depth, x=True, y=True, z=True):
        if x:
            for c in copies_x(e, depth):
                c.wait_recv()
        if z:
            copy_z(e).wait_recv()
        if y:
            up, down = copies_y(e)

            @pl.when(micro > 0)
            def _():
                up.wait_recv()

            @pl.when(micro < 3)
            def _():
                down.wait_recv()

    def drain(e, depth, x=True, y=True, z=True):
        if x:
            for c in copies_x(e, depth):
                c.wait_send()
        if z:
            copy_z(e).wait_send()
        if y:
            up, down = copies_y(e)

            @pl.when(micro < 3)
            def _():
                up.wait_send()

            @pl.when(micro > 0)
            def _():
                down.wait_send()

    def pack_plane(packed, plane, i, step=2):
        for q in range(TILES):
            n = i * TILES + q
            tile = plane[8 * q : 8 * q + 8]
            packed = jnp.where(pack_id[step] == n, pltpu.roll(tile, step * n, 1) if n else tile, packed)
        return packed

    def shifted_z(plane, message, i, step):
        tiles_up, tiles_down = [], []
        for q in range(TILES):
            n = i * TILES + q
            tile = plane[8 * q : 8 * q + 8]
            halo = pltpu.roll(message, NZ - step * n, 1) if n else message
            tiles_up.append(pltpu.roll(jnp.where(edge_up[step], halo, tile), NZ - step, 1))
            tiles_down.append(pltpu.roll(jnp.where(edge_down[step], halo, tile), step, 1))
        return jnp.concatenate(tiles_up, axis=0), jnp.concatenate(tiles_down, axis=0)

    def masked(plane, mask):
        return (plane.reshape(-1, 8, NZ) * mask).reshape(plane.shape)

    def put(e, i, plane):
        ex[e, 2 + i, inner, :] = plane

    def operator(e, write):
        message = zrecv[e]
        for i in range(NX):
            value = ex[e, 2 + i, inner, :]
            z_up, z_down = shifted_z(value, message, i, 2)
            total = coef[0, i] * value
            total -= coef[1, i] * ex[e, 4 + i, inner, :] + coef[2, i] * ex[e, i, inner, :]
            total -= coef[3, i] * ex[e, 2 + i, 10 : 10 + NY, :] + coef[4, i] * ex[e, 2 + i, 6 : 6 + NY, :]
            total -= coef[5, i] * z_up + coef[6, i] * z_down
            write(i, total)

    def red_copy(k, stage, step, peer, mine):
        n = stage * 16 + step
        return pltpu.make_async_remote_copy(
            src_ref=red.at[k, stage, mine], dst_ref=red.at[k, stage, mine],
            send_sem=red_send.at[k, n], recv_sem=red_recv.at[k, n], device_id=peer, device_id_type=MESH,
        )

    stages = ((peer_x, part_x, 8), (peer_blk, blk, 16))

    def red_start(k, stage, rows):
        peer, mine, count = stages[stage]
        red[k, stage, mine] = rows
        for step in range(1, count):
            red_copy(k, stage, step, peer(step), mine).start()

    def red_finish(k, stage):
        peer, mine, count = stages[stage]
        for step in range(1, count):
            red_copy(k, stage, step, peer(step), mine).wait_recv()
        total = red[k, stage, 0]
        for j in range(1, count):
            total = total + red[k, stage, j]
        return total

    def red_drain(k):
        for stage, (peer, mine, count) in enumerate(stages):
            for step in range(1, count):
                red_copy(k, stage, step, peer(step), mine).wait_send()

    def partial_dots():
        sums = [None] * N_DOT
        for i in range(NX):
            r, w, p, s, t = r_[i], w_[i], p_[i], s_[i], t_[i]
            kp = s + SIGMA * p
            kr = w + SIGMA * r
            kkp = (t + SIGMA * s) + SIGMA * kp
            terms = (
                r * r, r * kp, r * kr, r * kkp, kp * kp, kp * kr, kp * kkp,
                kr * kr, kr * kkp, kkp * kkp, p * kp, p * kr, p * kkp,
            )
            for j, term in enumerate(terms):
                folded = term.reshape(TILES, 8, NZ).sum(axis=0)
                sums[j] = folded if i == 0 else sums[j] + folded
        rows = [jnp.sum(a, axis=0, keepdims=True) for a in sums]
        rows = jnp.concatenate(rows + [jnp.zeros((16 - N_DOT, NZ), F32)], axis=0)
        sums = jnp.broadcast_to(jnp.sum(rows, axis=1, keepdims=True), (16, NZ))
        return jnp.sum(jnp.where(diagonal, sums, 0.0), axis=0, keepdims=True)

    def scalars(rows):
        d = jnp.sum(jnp.where(diagonal, jnp.broadcast_to(rows, (16, NZ)), 0.0), axis=1, keepdims=True)
        g = [d[j : j + 1, :] for j in range(N_DOT)]
        rr, rs, rw, rt, ss, sw, st, ww, wt, tt, ps, pw, pt = g
        alpha = rr / ps
        rr_1 = rr - 2.0 * alpha * rs + alpha * alpha * ss
        beta_1 = rr_1 / rr
        r_q = rw - alpha * rt + beta_1 * rs
        s_q = sw - alpha * st + beta_1 * ss
        p_q = pw - alpha * pt + beta_1 * ps
        alpha_1 = rr_1 / (r_q - alpha * s_q + beta_1 * p_q)
        w_q = ww - alpha * wt + beta_1 * sw
        t_q = wt - alpha * tt + beta_1 * st
        q_q = w_q - alpha * t_q + beta_1 * s_q
        rr_2 = rr_1 - 2.0 * alpha_1 * (r_q - alpha * s_q) + alpha_1 * alpha_1 * q_q
        beta_2 = rr_2 / rr_1
        return [jnp.broadcast_to(a, (NY, NZ)) for a in (alpha, beta_1, alpha_1, beta_2)]

    zeros = jnp.zeros((8, NZ), F32)

    def strains_at(i, top, count, halo):
        rows = pl.ds(8 + top, count)
        value = ex[E_DISP, 2 + i, rows, :]
        if halo is None:
            z_up, z_down = pltpu.roll(value, NZ - 1, 1), pltpu.roll(value, 1, 1)
        else:
            z_up, z_down = shifted_z(value, halo, i, 1)
        z_up, z_down = masked(z_up, keep_up_1), masked(z_down, keep_down_1)
        return (
            (ex[E_DISP, 3 + i, rows, :] - ex[E_DISP, 1 + i, rows, :]) * 0.5,
            (ex[E_DISP, 2 + i, 9 + top : 9 + top + count, :] - ex[E_DISP, 2 + i, 7 + top : 7 + top + count, :]) * 0.5,
            (z_up - z_down) * 0.5,
        )

    def store_points(base, count, strains, family, flag):
        rounded = [s.astype(BF16).astype(F32) for s in strains]
        rows = rounded + [s - h for s, h in zip(strains, rounded)] + [family, flag]
        for k, row in enumerate(rows):
            points[pl.ds(base + k, count, stride=8), :] = row

    def traits(i, top, count):
        family = lax.shift_right_logical(slot_ref[i, top : top + count, :], CAP_SHIFT).astype(F32)
        return family, flags_ref[i, top : top + count, :].astype(F32)

    def chunks(first, last, place):
        def chunk(j, carry):
            fibre_chunk(points, w_in, w_mid, w_out, [pl.multiple_of(base, 64) for base in place(j)])
            return carry

        lax.fori_loop(first, last, chunk, 0)

    middle = range(1, NX - 1)
    loads[0].wait()
    packed = zeros
    for i in range(NX):
        packed = pack_plane(packed, ex[E_DISP, 2 + i, inner, :], i, 1)
    zsend[E_DISP] = packed
    for c in loads[1:10]:
        c.wait()
    prepare_weights(fin_ref, fout_ref, ftan_ref, w_in, w_out)
    for i in middle:
        store_points((i * NY + 8) * 8, 16, strains_at(i, 8, 16, None), *traits(i, 8, 16))
    pl.semaphore_wait(barrier, len(friends))
    start(E_DISP, 1)

    def middle_rows(j):
        return j * (NY * 8) + 64, j * (NY * 8) + 128

    chunks(1, 4, middle_rows)
    finish(E_DISP, 1)
    message = zrecv[E_DISP]
    edges = [zeros] * 5
    for i in range(NX):
        strains = strains_at(i, 0, NY, message)
        family, flag = traits(i, 0, NY)
        columns = strains + (family, flag)
        edges = [pack_plane(e, c, i, 1) for e, c in zip(edges, columns)]
        for top in (0, 8, 16, 24):
            if i in (0, NX - 1) or top in (0, 24):
                part = [c[top : top + 8] for c in columns]
                store_points((i * NY + top) * 8, 8, part[:3], part[3], part[4])
    store_points(FIX, 8, edges[:3], edges[3], edges[4])
    fibre_chunk(points, w_in, w_mid, w_out, [FIX])

    def face_rows(j):
        base = lax.div(j, 2) * ((NX - 1) * NY * 8) + lax.rem(j, 2) * 128
        return base, base + 64

    def side_rows(j):
        return j * (NY * 8), j * (NY * 8) + 192

    chunks(0, 4, face_rows)
    chunks(1, NX - 1, side_rows)

    def results(base, count):
        sx, sy, sz, high, low = [points[pl.ds(base + k, count, stride=8), :] for k in range(5)]
        return sx, sy, sz, 0.5 + (high + low)

    def keep_results(i, top, count, values):
        rows = pl.ds(8 + top, count)
        ex[E_SX, 2 + i, rows, :] = values[0]
        ex[E_SY, 2 + i, rows, :] = values[1]
        s_z[i, pl.ds(top, count), :] = values[2]
        ex[E_TAN, 2 + i, rows, :] = values[3]

    edges = results(FIX, 8)
    zsend[E_SX] = edges[2]
    zsend[E_TAN] = edges[3]
    for i in range(NX):
        for top, count in ((0, NY),) if i in (0, NX - 1) else ((0, 8), (24, 8)):
            keep_results(i, top, count, results((i * NY + top) * 8, count))
    start(E_SX, 1, y=False)
    start(E_TAN, 1)
    start(E_SY, 1, x=False, z=False)
    chunks(4, NX - 1, middle_rows)
    for i in middle:
        for top in (8, 16):
            n = i * TILES + top // 8
            values = results((i * NY + top) * 8, 8)
            values = [jnp.where(edge_own, pltpu.roll(e, NZ - n, 1), v) for e, v in zip(edges, values)]
            keep_results(i, top, 8, values)

    loads[10].wait()
    loads[11].wait()
    finish(E_SX, 1, y=False)
    finish(E_TAN, 1)
    finish(E_SY, 1, x=False, z=False)
    message_s, message_t = zrecv[E_SX], zrecv[E_TAN]
    packed = jnp.zeros((8, NZ), F32)
    for i in range(NX):
        up, down = shifted_z(s_z[i], message_s, i, 1)
        total = (ex[E_SX, 3 + i, inner, :] - ex[E_SX, 1 + i, inner, :]) * 0.5
        total += (ex[E_SY, 2 + i, 9 : 9 + NY, :] - ex[E_SY, 2 + i, 7 : 7 + NY, :]) * 0.5
        total += (masked(up, keep_up_1) - masked(down, keep_down_1)) * 0.5
        rhs = load_ref[i] - found_ref[i] * ex[E_DISP, 2 + i, inner, :] + total
        put(E_R, i, rhs)
        packed = pack_plane(packed, rhs, i)
        r_[i] = rhs
        p_[i] = rhs
        x_[i] = jnp.zeros((NY, NZ), F32)
        u_[i] = jnp.zeros((NY, NZ), F32)
    zsend[E_R] = packed
    start(E_R, 2)
    for i in range(NX):
        up, down = shifted_z(ex[E_TAN, 2 + i, inner, :], message_t, i, 1)
        z_up, z_down = masked(up, keep_up_1) * 0.25, masked(down, keep_down_1) * 0.25
        x_up, x_down = ex[E_TAN, 3 + i, inner, :] * 0.25, ex[E_TAN, 1 + i, inner, :] * 0.25
        y_up, y_down = ex[E_TAN, 2 + i, 9 : 9 + NY, :] * 0.25, ex[E_TAN, 2 + i, 7 : 7 + NY, :] * 0.25
        coef[0, i] = found_ref[i] + ((x_up + x_down) + (y_up + y_down) + (z_up + z_down)) - SIGMA
        coef[1, i], coef[2, i] = x_up, x_down
        coef[3, i], coef[4, i] = y_up, y_down
        coef[5, i], coef[6, i] = masked(z_up, keep_up_2), masked(z_down, keep_down_2)

    class Packer:
        def __init__(self):
            self.packed = jnp.zeros((8, NZ), F32)

        def add(self, plane, i):
            self.packed = pack_plane(self.packed, plane, i)

    finish(E_R, 2)
    pack = Packer()

    def write_w(i, value):
        put(E_W, i, value)
        w_[i] = value
        s_[i] = value
        pack.add(value, i)

    operator(E_R, write_w)
    zsend[E_W] = pack.packed
    start(E_W, 2)
    finish(E_W, 2)
    pack_t = Packer()

    def write_z(i, value):
        put(E_T, i, value)
        z_[i] = value
        t_[i] = value
        pack_t.add(value, i)

    operator(E_W, write_z)
    zsend[E_T] = pack_t.packed

    def block(k, beta):
        e_t, e_u = E_T + 2 * k, E_T + 2 * k + 1
        start(e_t, 2)
        red_start(k, 0, partial_dots())
        red_start(k, 1, red_finish(k, 0))
        finish(e_t, 2)
        pack_u = Packer()

        def write_u(i, value):
            put(e_u, i, value)
            z2_[i] = value - beta * u_[i]
            u_[i] = value
            pack_u.add(value, i)

        operator(e_t, write_u)
        zsend[e_u] = pack_u.packed
        start(e_u, 2)
        finish(e_u, 2)

        def write_v(i, value):
            v_[i] = value

        operator(e_u, write_v)
        alpha, beta_1, alpha_1, beta_2 = scalars(red_finish(k, 1))
        pack_n = Packer()
        tangents = []
        for i in range(NX):
            p, s, t, u = p_[i], s_[i], t_[i], u_[i]
            x = x_[i] + alpha * p
            r = r_[i] - alpha * (s + SIGMA * p)
            w = w_[i] - alpha * (t + SIGMA * s)
            z = z_[i] - alpha * (u + SIGMA * t)
            z2 = z2_[i] - alpha * (v_[i] + SIGMA * u)
            p = r + beta_1 * p
            s = w + beta_1 * s
            t = z + beta_1 * t
            u = z2 + beta_1 * u
            x_[i] = x + alpha_1 * p
            r = r - alpha_1 * (s + SIGMA * p)
            w = w - alpha_1 * (t + SIGMA * s)
            z = z - alpha_1 * (u + SIGMA * t)
            r_[i], w_[i], z_[i], u_[i] = r, w, z, u
            p_[i] = r + beta_2 * p
            s_[i] = w + beta_2 * s
            t = z + beta_2 * t
            t_[i] = t
            tangents.append(t)
        for i in range(NX):
            pack_n.add(tangents[i], i)

        @pl.when(k < 2)
        def _():
            for i in range(NX):
                put(e_t + 2, i, tangents[i])
            zsend[e_t + 2] = pack_n.packed

        return beta_2

    lax.fori_loop(0, 3, block, jnp.zeros((NY, NZ), F32))

    last = N_RED - 1
    red_start(last, 0, partial_dots())
    red_start(last, 1, red_finish(last, 0))
    alpha, beta_1, alpha_1, _ = scalars(red_finish(last, 1))
    for i in range(NX):
        p, s, t = p_[i], s_[i], t_[i]
        x = x_[i] + alpha * p
        r = r_[i] - alpha * (s + SIGMA * p)
        w = w_[i] - alpha * (t + SIGMA * s)
        p = r + beta_1 * p
        s = w + beta_1 * s
        field_out[i] = ex[E_DISP, 2 + i, inner, :] + (x + alpha_1 * p)
        residual_out[i] = r - alpha_1 * (s + SIGMA * p)

    drain(E_DISP, 1)
    drain(E_SX, 1, y=False)
    drain(E_TAN, 1)
    drain(E_SY, 1, x=False, z=False)

    def drain_step(e, carry):
        drain(e, 2)
        return carry

    lax.fori_loop(E_R, N_EX, drain_step, 0)

    def drain_red(k, carry):
        red_drain(k)
        return carry

    lax.fori_loop(0, N_RED, drain_red, 0)


def body(displacement, load_field, foundation, flags, slots, family_in, family_mid, family_out, family_tan):
    family_in, family_out = jnp.transpose(family_in, (1, 0, 2)), jnp.transpose(family_out, (1, 0, 2))
    shape = (NX, NY, NZ)
    field = pltpu.VMEM(shape, F32)
    ints = pltpu.VMEM(shape, jnp.int32)
    whole = pl.BlockSpec(memory_space=pltpu.VMEM)
    return pl.pallas_call(
        newton_kernel,
        out_shape=(jax.ShapeDtypeStruct(shape, F32), jax.ShapeDtypeStruct(shape, F32)),
        in_specs=[pl.BlockSpec(memory_space=pl.ANY)] * 9,
        out_specs=(whole, whole),
        scratch_shapes=[
            field,
            field,
            ints,
            ints,
            pltpu.VMEM((3, FAMILIES, MODES), F32),
            pltpu.VMEM((3, FAMILIES, MODES), BF16),
            pltpu.VMEM((FAMILIES, MODES), F32),
            pltpu.VMEM((N_EX, NX + 4, NY + 16, NZ), F32),
            pltpu.VMEM((N_EX, 8, NZ), F32),
            pltpu.VMEM((N_EX, 8, NZ), F32),
            pltpu.VMEM((N_RED, 2, 16, 1, NZ), F32),
            pltpu.VMEM((FIX + 64, NZ), F32),
            pltpu.VMEM((MODES, 64), BF16),
            pltpu.VMEM((MODES, FAMILIES * MODES), BF16),
            pltpu.VMEM((32, 2 * MODES), BF16),
            pltpu.VMEM((7,) + shape, F32),
            field,
        ]
        + [field] * 10
        + [
            pltpu.SemaphoreType.DMA((N_EX, 5)),
            pltpu.SemaphoreType.DMA((N_EX, 5)),
            pltpu.SemaphoreType.DMA((N_RED, 32)),
            pltpu.SemaphoreType.DMA((N_RED, 32)),
            pltpu.SemaphoreType.DMA((N_IN,)),
        ],
        compiler_params=pltpu.CompilerParams(
            collective_id=0, has_side_effects=True, vmem_limit_bytes=60 * 1024 * 1024
        ),
        name="newton_step",
    )(displacement, load_field, foundation, flags, slots, family_in, family_mid, family_out, family_tan)


def solution(mesh):
    placed = P("blk", "micro", "slab")
    return jax.shard_map(
        body,
        mesh=mesh,
        in_specs=(placed,) * 5 + (P(),) * 4,
        out_specs=(placed, placed),
        check_vma=False,
    )
```

```python
import jax
import jax.numpy as jnp
from jax import lax
from jax.experimental import pallas as pl
from jax.experimental.pallas import tpu as pltpu
from jax.sharding import PartitionSpec as P

F32 = jnp.float32
BF16 = jnp.bfloat16
MESH = pl.DeviceIdType.MESH
FAMILIES = 4
MODES = 256
CAP_SHIFT = 14
SIGMA = 3.0
NX, NY, NZ = 8, 32, 128
TILES = NY // 8
E_DISP, E_TAN, E_SX, E_SY, E_R, E_W, E_T = 0, 1, 2, 3, 4, 5, 6
N_EX = 12
INSIDE = (2, 3, 4, 5)
OUTSIDE = (0, 1, 6, 7)
N_RED = 4
N_IN = 12
FIX = NX * NY * 8
N_DOT = 13


def prepare_weights(family_in, family_out, family_tan, w_in, w_out):
    zero = jnp.zeros((1, MODES), F32)
    high, low, stress, tangent = [], [], [], []
    for f in range(FAMILIES):
        weight = family_in[:, f, :]
        rounded = weight.astype(BF16).astype(F32)
        high += [rounded, rounded, zero, zero]
        low += [weight - rounded, zero, zero, zero, zero, zero]
        tan = family_tan[f : f + 1, :]
        tan_high = tan.astype(BF16).astype(F32)
        stress += [family_out[:, f, :].astype(F32)] + [zero] * 5
        tangent += [zero] * 3 + [tan_high, tan - tan_high] + [zero] * 3
    w_in[...] = jnp.concatenate(high + low, axis=0).T.astype(BF16)
    w_out[:, :MODES] = jnp.concatenate(stress, axis=0).astype(BF16)
    w_out[:, MODES:] = jnp.concatenate(tangent, axis=0).astype(BF16)


def fibre_chunk(points, w_in, w_mid, w_out, bases):
    places = [base + 8 * i for base in bases for i in range(8)]
    width = len(places) * NZ
    rows = jnp.concatenate([points[pl.ds(place, 8), :] for place in places], axis=1)
    family, flag = rows[6:7, :], rows[7:8, :]
    family_8 = jnp.broadcast_to(family, (8, width))
    chosen = [family_8 == float(f) for f in range(FAMILIES)]
    strain = jnp.concatenate([jnp.where(m, rows, 0.0) for m in chosen], axis=0).astype(BF16)
    modal = jnp.dot(w_in[...], jnp.concatenate([strain, strain], axis=0), preferred_element_type=F32)
    modal = modal.reshape(MODES // 8, 8, width)
    plastic = jnp.broadcast_to(flag, (8, width)) > 0.5
    active = jnp.where(plastic[None], jnp.tanh(modal), modal).reshape(MODES, width).astype(BF16)
    active = active.reshape(MODES // 16, 16, width)
    family_16 = jnp.broadcast_to(family, (16, width))
    parts = []
    for f in range(FAMILIES):
        mask = jnp.where(family_16 == float(f), 1.0, 0.0).astype(BF16)
        parts.append((active * mask[None]).reshape(MODES, width))
    hidden = jnp.dot(w_mid[...], jnp.concatenate(parts, axis=0), preferred_element_type=F32)
    bounded = jnp.tanh(hidden).astype(BF16)
    out = jnp.dot(
        w_out[...], jnp.concatenate([bounded, bounded * bounded], axis=0), preferred_element_type=F32
    )
    picked = jnp.where(
        chosen[0], out[0:8], jnp.where(chosen[1], out[8:16], jnp.where(chosen[2], out[16:24], out[24:32]))
    )
    for i, place in enumerate(places):
        points[pl.ds(place, 8), :] = picked[:, i * NZ : (i + 1) * NZ]


def newton_kernel(
    disp_hbm, load_hbm, found_hbm, flags_hbm, slot_hbm, fin_hbm, fmid_hbm, fout_hbm, ftan_hbm,
    gain_out, residual_out, change_out,
    load_ref, found_ref, flags_ref, slot_ref, fin_ref, fout_ref, ftan_ref,
    ex, zsend, zrecv, red, points, w_in, w_mid, w_out, coef, s_z,
    x_, r_, w_, z_, z2_, p_, s_, t_, u_, v_,
    send_sem, recv_sem, red_send, red_recv, in_sem,
):
    inner = pl.ds(8, NY)
    pairs = [(disp_hbm, ex.at[E_DISP, pl.ds(2, NX), inner, :]), (slot_hbm, slot_ref), (flags_hbm, flags_ref)]
    pairs += [(fin_hbm, fin_ref), (fout_hbm, fout_ref), (ftan_hbm, ftan_ref)]
    pairs += [(fmid_hbm.at[f], w_mid.at[:, pl.ds(f * MODES, MODES)]) for f in range(FAMILIES)]
    pairs += [(found_hbm, found_ref), (load_hbm, load_ref)]
    loads = [pltpu.make_async_copy(a, b, in_sem.at[j]) for j, (a, b) in enumerate(pairs)]
    for c in loads:
        c.start()
    blk, slab, micro = lax.axis_index("blk"), lax.axis_index("slab"), lax.axis_index("micro")
    n_blk = lax.axis_size("blk")
    up_blk, down_blk = lax.rem(blk + 1, n_blk), lax.rem(blk + n_blk - 1, n_blk)
    part_x = slab * 4 + micro

    def peer_x(step):
        other = lax.rem(part_x + step, 8)
        return (blk, lax.div(other, 4), lax.rem(other, 4))

    def peer_blk(step):
        return (lax.rem(blk + step, n_blk), slab, micro)

    barrier = pltpu.get_barrier_semaphore()
    friends = [peer_x(j) for j in range(1, 8)] + [peer_blk(j) for j in range(1, 16)]
    for friend in friends:
        pl.semaphore_signal(barrier, inc=1, device_id=friend, device_id_type=MESH)

    lane = lax.broadcasted_iota(jnp.int32, (8, NZ), 1)
    diagonal = lax.broadcasted_iota(jnp.int32, (16, NZ), 0) == lax.broadcasted_iota(jnp.int32, (16, NZ), 1)
    first_slab, last_slab = slab == 0, slab == 1
    pack_id = {n: lax.div(lax.rem(lane + n * (1 - slab), NZ), n) for n in (1, 2)}
    edge_own = jnp.logical_or(jnp.logical_and(lane == NZ - 1, slab == 0), jnp.logical_and(lane == 0, slab == 1))
    edge_up = {n: jnp.logical_and(lane < n, first_slab) for n in (1, 2)}
    edge_down = {n: jnp.logical_and(lane >= NZ - n, last_slab) for n in (1, 2)}

    def keep(condition):
        return jnp.where(condition, 0.0, 1.0).astype(F32)

    keep_up_1 = keep(jnp.logical_and(lane == NZ - 1, last_slab))[None]
    keep_down_1 = keep(jnp.logical_and(lane == 0, first_slab))[None]
    keep_up_2 = keep(jnp.logical_and(lane >= NZ - 2, last_slab))[None]
    keep_down_2 = keep(jnp.logical_and(lane < 2, first_slab))[None]

    @pl.when(micro == 0)
    def _():
        for e in range(N_EX):
            ex[e, :, 0:8, :] = jnp.zeros((NX + 4, 8, NZ), F32)

    @pl.when(micro == 3)
    def _():
        for e in range(N_EX):
            ex[e, :, NY + 8 : NY + 16, :] = jnp.zeros((NX + 4, 8, NZ), F32)

    def copy(source, target, e, k, device):
        return pltpu.make_async_remote_copy(
            src_ref=source, dst_ref=target, send_sem=send_sem.at[e, k], recv_sem=recv_sem.at[e, k],
            device_id=device, device_id_type=MESH,
        )

    def copies_x(e, depth):
        up = copy(
            ex.at[e, pl.ds(NX + 2 - depth, depth), pl.ds(8, NY), :],
            ex.at[e, pl.ds(2 - depth, depth), pl.ds(8, NY), :], e, 0, (up_blk, slab, micro),
        )
        down = copy(
            ex.at[e, pl.ds(2, depth), pl.ds(8, NY), :],
            ex.at[e, pl.ds(NX + 2, depth), pl.ds(8, NY), :], e, 1, (down_blk, slab, micro),
        )
        return up, down

    def copies_y(e):
        up = copy(
            ex.at[e, pl.ds(2, NX), pl.ds(NY, 8), :], ex.at[e, pl.ds(2, NX), pl.ds(0, 8), :],
            e, 2, (blk, slab, lax.rem(micro + 1, 4)),
        )
        down = copy(
            ex.at[e, pl.ds(2, NX), pl.ds(8, 8), :], ex.at[e, pl.ds(2, NX), pl.ds(NY + 8, 8), :],
            e, 3, (blk, slab, lax.rem(micro + 3, 4)),
        )
        return up, down

    def copy_z(e):
        return copy(zsend.at[e], zrecv.at[e], e, 4, (blk, 1 - slab, micro))

    def start(e, depth, x=True, y=True, z=True):
        if x:
            for c in copies_x(e, depth):
                c.start()
        if z:
            copy_z(e).start()
        if y:
            up, down = copies_y(e)

            @pl.when(micro < 3)
            def _():
                up.start()

            @pl.when(micro > 0)
            def _():
                down.start()

    def finish(e, depth, x=True, y=True, z=True):
        if x:
            for c in copies_x(e, depth):
                c.wait_recv()
        if z:
            copy_z(e).wait_recv()
        if y:
            up, down = copies_y(e)

            @pl.when(micro > 0)
            def _():
                up.wait_recv()

            @pl.when(micro < 3)
            def _():
                down.wait_recv()

    def drain(e, depth, x=True, y=True, z=True):
        if x:
            for c in copies_x(e, depth):
                c.wait_send()
        if z:
            copy_z(e).wait_send()
        if y:
            up, down = copies_y(e)

            @pl.when(micro < 3)
            def _():
                up.wait_send()

            @pl.when(micro > 0)
            def _():
                down.wait_send()

    def pack_plane(packed, plane, i, step=2):
        for q in range(TILES):
            n = i * TILES + q
            tile = plane[8 * q : 8 * q + 8]
            packed = jnp.where(pack_id[step] == n, pltpu.roll(tile, step * n, 1) if n else tile, packed)
        return packed

    def shifted_z(plane, message, i, step):
        tiles_up, tiles_down = [], []
        for q in range(TILES):
            n = i * TILES + q
            tile = plane[8 * q : 8 * q + 8]
            halo = pltpu.roll(message, NZ - step * n, 1) if n else message
            tiles_up.append(pltpu.roll(jnp.where(edge_up[step], halo, tile), NZ - step, 1))
            tiles_down.append(pltpu.roll(jnp.where(edge_down[step], halo, tile), step, 1))
        return jnp.concatenate(tiles_up, axis=0), jnp.concatenate(tiles_down, axis=0)

    def masked(plane, mask):
        return (plane.reshape(-1, 8, NZ) * mask).reshape(plane.shape)

    def put(e, i, plane):
        ex[e, 2 + i, inner, :] = plane

    def operator(e, planes, write):
        message = zrecv[e]
        for i in planes:
            value = ex[e, 2 + i, inner, :]
            z_up, z_down = shifted_z(value, message, i, 2)
            total = coef[0, i] * value
            total -= coef[1, i] * ex[e, 4 + i, inner, :] + coef[2, i] * ex[e, i, inner, :]
            total -= coef[3, i] * ex[e, 2 + i, 10 : 10 + NY, :] + coef[4, i] * ex[e, 2 + i, 6 : 6 + NY, :]
            total -= coef[5, i] * z_up + coef[6, i] * z_down
            write(i, total)

    def red_copy(k, stage, step, peer, mine):
        n = stage * 16 + step
        return pltpu.make_async_remote_copy(
            src_ref=red.at[k, stage, mine], dst_ref=red.at[k, stage, mine],
            send_sem=red_send.at[k, n], recv_sem=red_recv.at[k, n], device_id=peer, device_id_type=MESH,
        )

    stages = ((peer_x, part_x, 8), (peer_blk, blk, 16))

    def red_start(k, stage, rows):
        peer, mine, count = stages[stage]
        red[k, stage, mine] = rows
        for step in range(1, count):
            red_copy(k, stage, step, peer(step), mine).start()

    def red_finish(k, stage):
        peer, mine, count = stages[stage]
        for step in range(1, count):
            red_copy(k, stage, step, peer(step), mine).wait_recv()
        total = red[k, stage, 0]
        for j in range(1, count):
            total = total + red[k, stage, j]
        return total

    def red_drain(k):
        for stage, (peer, mine, count) in enumerate(stages):
            for step in range(1, count):
                red_copy(k, stage, step, peer(step), mine).wait_send()

    def add_dots(sums, r, w, p, s, t):
        kp = s + SIGMA * p
        kr = w + SIGMA * r
        kkp = (t + SIGMA * s) + SIGMA * kp
        terms = (
            r * r, r * kp, r * kr, r * kkp, kp * kp, kp * kr, kp * kkp,
            kr * kr, kr * kkp, kkp * kkp, p * kp, p * kr, p * kkp,
        )
        folded = [term.reshape(TILES, 8, NZ).sum(axis=0) for term in terms]
        return folded if sums is None else [a + b for a, b in zip(sums, folded)]

    def row_of(sums):
        rows = [jnp.sum(a, axis=0, keepdims=True) for a in sums]
        rows = jnp.concatenate(rows + [jnp.zeros((16 - N_DOT, NZ), F32)], axis=0)
        sums = jnp.broadcast_to(jnp.sum(rows, axis=1, keepdims=True), (16, NZ))
        return jnp.sum(jnp.where(diagonal, sums, 0.0), axis=0, keepdims=True)

    def scalars(rows):
        d = jnp.sum(jnp.where(diagonal, jnp.broadcast_to(rows, (16, NZ)), 0.0), axis=1, keepdims=True)
        g = [d[j : j + 1, :] for j in range(N_DOT)]
        rr, rs, rw, rt, ss, sw, st, ww, wt, tt, ps, pw, pt = g
        alpha = rr / ps
        rr_1 = rr - 2.0 * alpha * rs + alpha * alpha * ss
        beta_1 = rr_1 / rr
        r_q = rw - alpha * rt + beta_1 * rs
        s_q = sw - alpha * st + beta_1 * ss
        p_q = pw - alpha * pt + beta_1 * ps
        alpha_1 = rr_1 / (r_q - alpha * s_q + beta_1 * p_q)
        w_q = ww - alpha * wt + beta_1 * sw
        t_q = wt - alpha * tt + beta_1 * st
        q_q = w_q - alpha * t_q + beta_1 * s_q
        rr_2 = rr_1 - 2.0 * alpha_1 * (r_q - alpha * s_q) + alpha_1 * alpha_1 * q_q
        beta_2 = rr_2 / rr_1
        return [jnp.broadcast_to(a, (NY, NZ)) for a in (alpha, beta_1, alpha_1, beta_2)]

    zeros = jnp.zeros((8, NZ), F32)

    def strains_at(i, top, count, halo):
        rows = pl.ds(8 + top, count)
        value = ex[E_DISP, 2 + i, rows, :]
        if halo is None:
            z_up, z_down = pltpu.roll(value, NZ - 1, 1), pltpu.roll(value, 1, 1)
        else:
            z_up, z_down = shifted_z(value, halo, i, 1)
        z_up, z_down = masked(z_up, keep_up_1), masked(z_down, keep_down_1)
        return (
            (ex[E_DISP, 3 + i, rows, :] - ex[E_DISP, 1 + i, rows, :]) * 0.5,
            (ex[E_DISP, 2 + i, 9 + top : 9 + top + count, :] - ex[E_DISP, 2 + i, 7 + top : 7 + top + count, :]) * 0.5,
            (z_up - z_down) * 0.5,
        )

    def store_points(base, count, strains, family, flag):
        rounded = [s.astype(BF16).astype(F32) for s in strains]
        rows = rounded + [s - h for s, h in zip(strains, rounded)] + [family, flag]
        for k, row in enumerate(rows):
            points[pl.ds(base + k, count, stride=8), :] = row

    def traits(i, top, count):
        family = lax.shift_right_logical(slot_ref[i, top : top + count, :], CAP_SHIFT).astype(F32)
        return family, flags_ref[i, top : top + count, :].astype(F32)

    def chunks(first, last, place):
        def chunk(j, carry):
            fibre_chunk(points, w_in, w_mid, w_out, [pl.multiple_of(base, 64) for base in place(j)])
            return carry

        lax.fori_loop(first, last, chunk, 0)

    middle = range(1, NX - 1)
    loads[0].wait()
    packed = zeros
    for i in range(NX):
        packed = pack_plane(packed, ex[E_DISP, 2 + i, inner, :], i, 1)
    zsend[E_DISP] = packed
    for c in loads[1:10]:
        c.wait()
    prepare_weights(fin_ref, fout_ref, ftan_ref, w_in, w_out)
    for i in middle:
        store_points((i * NY + 8) * 8, 16, strains_at(i, 8, 16, None), *traits(i, 8, 16))
    pl.semaphore_wait(barrier, len(friends))
    start(E_DISP, 1)

    def middle_rows(j):
        return j * (NY * 8) + 64, j * (NY * 8) + 128

    chunks(1, 4, middle_rows)
    finish(E_DISP, 1)
    message = zrecv[E_DISP]
    edges = [zeros] * 5
    for i in range(NX):
        strains = strains_at(i, 0, NY, message)
        family, flag = traits(i, 0, NY)
        columns = strains + (family, flag)
        edges = [pack_plane(e, c, i, 1) for e, c in zip(edges, columns)]
        for top in (0, 8, 16, 24):
            if i in (0, NX - 1) or top in (0, 24):
                part = [c[top : top + 8] for c in columns]
                store_points((i * NY + top) * 8, 8, part[:3], part[3], part[4])
    store_points(FIX, 8, edges[:3], edges[3], edges[4])
    fibre_chunk(points, w_in, w_mid, w_out, [FIX])

    def face_rows(j):
        base = lax.div(j, 2) * ((NX - 1) * NY * 8) + lax.rem(j, 2) * 128
        return base, base + 64

    def side_rows(j):
        return j * (NY * 8), j * (NY * 8) + 192

    chunks(0, 4, face_rows)
    chunks(1, NX - 1, side_rows)

    def results(base, count):
        sx, sy, sz, high, low = [points[pl.ds(base + k, count, stride=8), :] for k in range(5)]
        return sx, sy, sz, 0.5 + (high + low)

    def keep_results(i, top, count, values):
        rows = pl.ds(8 + top, count)
        ex[E_SX, 2 + i, rows, :] = values[0]
        ex[E_SY, 2 + i, rows, :] = values[1]
        s_z[i, pl.ds(top, count), :] = values[2]
        ex[E_TAN, 2 + i, rows, :] = values[3]

    edges = results(FIX, 8)
    zsend[E_SX] = edges[2]
    zsend[E_TAN] = edges[3]
    for i in range(NX):
        for top, count in ((0, NY),) if i in (0, NX - 1) else ((0, 8), (24, 8)):
            keep_results(i, top, count, results((i * NY + top) * 8, count))
    start(E_SX, 1, y=False)
    start(E_TAN, 1)
    start(E_SY, 1, x=False, z=False)
    chunks(4, NX - 1, middle_rows)
    for i in middle:
        for top in (8, 16):
            n = i * TILES + top // 8
            values = results((i * NY + top) * 8, 8)
            values = [jnp.where(edge_own, pltpu.roll(e, NZ - n, 1), v) for e, v in zip(edges, values)]
            keep_results(i, top, 8, values)

    loads[10].wait()
    loads[11].wait()
    finish(E_SX, 1, y=False)
    finish(E_TAN, 1)
    finish(E_SY, 1, x=False, z=False)
    message_s, message_t = zrecv[E_SX], zrecv[E_TAN]
    packed = zeros
    for i in OUTSIDE + INSIDE:
        up, down = shifted_z(s_z[i], message_s, i, 1)
        total = (ex[E_SX, 3 + i, inner, :] - ex[E_SX, 1 + i, inner, :]) * 0.5
        total += (ex[E_SY, 2 + i, 9 : 9 + NY, :] - ex[E_SY, 2 + i, 7 : 7 + NY, :]) * 0.5
        total += (masked(up, keep_up_1) - masked(down, keep_down_1)) * 0.5
        rhs = load_ref[i] - found_ref[i] * ex[E_DISP, 2 + i, inner, :] + total
        put(E_R, i, rhs)
        packed = pack_plane(packed, rhs, i)
        r_[i] = rhs
        p_[i] = rhs
        x_[i] = jnp.zeros((NY, NZ), F32)
        u_[i] = jnp.zeros((NY, NZ), F32)
        if i == OUTSIDE[-1]:
            start(E_R, 2, y=False, z=False)
    zsend[E_R] = packed
    start(E_R, 2, x=False)
    for i in range(NX):
        up, down = shifted_z(ex[E_TAN, 2 + i, inner, :], message_t, i, 1)
        z_up, z_down = masked(up, keep_up_1) * 0.25, masked(down, keep_down_1) * 0.25
        x_up, x_down = ex[E_TAN, 3 + i, inner, :] * 0.25, ex[E_TAN, 1 + i, inner, :] * 0.25
        y_up, y_down = ex[E_TAN, 2 + i, 9 : 9 + NY, :] * 0.25, ex[E_TAN, 2 + i, 7 : 7 + NY, :] * 0.25
        coef[0, i] = found_ref[i] + ((x_up + x_down) + (y_up + y_down) + (z_up + z_down)) - SIGMA
        coef[1, i], coef[2, i] = x_up, x_down
        coef[3, i], coef[4, i] = y_up, y_down
        coef[5, i], coef[6, i] = masked(z_up, keep_up_2), masked(z_down, keep_down_2)

    def step(e, target, write, between=lambda: None):
        box = [zeros]

        def store(i, value):
            put(target, i, value)
            write(i, value)
            box[0] = pack_plane(box[0], value, i)

        finish(e, 2, x=False)
        operator(e, INSIDE, store)
        between()
        finish(e, 2, y=False, z=False)
        operator(e, OUTSIDE, store)
        start(target, 2, y=False, z=False)
        zsend[target] = box[0]
        start(target, 2, x=False)

    def write_w(i, value):
        w_[i] = value
        s_[i] = value

    def write_z(i, value):
        z_[i] = value
        t_[i] = value

    step(E_R, E_W, write_w)
    step(E_W, E_T, write_z)
    sums = None
    for i in range(NX):
        sums = add_dots(sums, r_[i], w_[i], p_[i], s_[i], t_[i])
    red_start(0, 0, row_of(sums))

    def block(k, beta):
        e_t, e_u = E_T + 2 * k, E_T + 2 * k + 1

        def write_u(i, value):
            z2_[i] = value - beta * u_[i]
            u_[i] = value

        step(e_t, e_u, write_u, lambda: red_start(k, 1, red_finish(k, 0)))

        def write_v(i, value):
            v_[i] = value

        finish(e_u, 2, x=False)
        operator(e_u, INSIDE, write_v)
        alpha, beta_1, alpha_1, beta_2 = scalars(red_finish(k, 1))
        box = [zeros]
        sums = None

        def update(i):
            p, s, t, u = p_[i], s_[i], t_[i], u_[i]
            x = x_[i] + alpha * p
            r = r_[i] - alpha * (s + SIGMA * p)
            w = w_[i] - alpha * (t + SIGMA * s)
            z = z_[i] - alpha * (u + SIGMA * t)
            z2 = z2_[i] - alpha * (v_[i] + SIGMA * u)
            p = r + beta_1 * p
            s = w + beta_1 * s
            t = z + beta_1 * t
            u = z2 + beta_1 * u
            x_[i] = x + alpha_1 * p
            r = r - alpha_1 * (s + SIGMA * p)
            w = w - alpha_1 * (t + SIGMA * s)
            z = z - alpha_1 * (u + SIGMA * t)
            r_[i], w_[i], z_[i], u_[i] = r, w, z, u
            p = r + beta_2 * p
            s = w + beta_2 * s
            t = z + beta_2 * t
            p_[i], s_[i], t_[i] = p, s, t
            put(e_t + 2, i, t)
            box[0] = pack_plane(box[0], t, i)

        for i in INSIDE:
            update(i)
            sums = add_dots(sums, r_[i], w_[i], p_[i], s_[i], t_[i])
        finish(e_u, 2, y=False, z=False)
        operator(e_u, OUTSIDE, write_v)
        for i in OUTSIDE:
            update(i)

        @pl.when(k < 2)
        def _():
            start(e_t + 2, 2, y=False, z=False)
            zsend[e_t + 2] = box[0]
            start(e_t + 2, 2, x=False)

        for i in OUTSIDE:
            sums = add_dots(sums, r_[i], w_[i], p_[i], s_[i], t_[i])
        red_start(k + 1, 0, row_of(sums))
        return beta_2

    lax.fori_loop(0, 3, block, jnp.zeros((NY, NZ), F32))

    last = N_RED - 1
    red_start(last, 1, red_finish(last, 0))
    alpha, beta_1, alpha_1, _ = scalars(red_finish(last, 1))
    for i in range(NX):
        p, s, t = p_[i], s_[i], t_[i]
        x = x_[i] + alpha * p
        r = r_[i] - alpha * (s + SIGMA * p)
        w = w_[i] - alpha * (t + SIGMA * s)
        p = r + beta_1 * p
        s = w + beta_1 * s
        gain_out[i] = x + alpha_1 * p
        residual_out[i] = r
        change_out[i] = alpha_1 * (s + SIGMA * p)

    drain(E_DISP, 1)
    drain(E_SX, 1, y=False)
    drain(E_TAN, 1)
    drain(E_SY, 1, x=False, z=False)

    def drain_step(e, carry):
        drain(e, 2)
        return carry

    lax.fori_loop(E_R, N_EX, drain_step, 0)

    def drain_red(k, carry):
        red_drain(k)
        return carry

    lax.fori_loop(0, N_RED, drain_red, 0)


def body(displacement, load_field, foundation, flags, slots, family_in, family_mid, family_out, family_tan):
    family_in, family_out = jnp.transpose(family_in, (1, 0, 2)), jnp.transpose(family_out, (1, 0, 2))
    shape = (NX, NY, NZ)
    field = pltpu.VMEM(shape, F32)
    ints = pltpu.VMEM(shape, jnp.int32)
    whole = pl.BlockSpec(memory_space=pltpu.VMEM)
    gain, residual, change = pl.pallas_call(
        newton_kernel,
        out_shape=(jax.ShapeDtypeStruct(shape, F32),) * 3,
        in_specs=[pl.BlockSpec(memory_space=pl.ANY)] * 9,
        out_specs=(whole,) * 3,
        scratch_shapes=[
            field,
            field,
            ints,
            ints,
            pltpu.VMEM((3, FAMILIES, MODES), F32),
            pltpu.VMEM((3, FAMILIES, MODES), BF16),
            pltpu.VMEM((FAMILIES, MODES), F32),
            pltpu.VMEM((N_EX + 1, NX + 4, NY + 16, NZ), F32),
            pltpu.VMEM((N_EX, 8, NZ), F32),
            pltpu.VMEM((N_EX, 8, NZ), F32),
            pltpu.VMEM((N_RED, 2, 16, 1, NZ), F32),
            pltpu.VMEM((FIX + 64, NZ), F32),
            pltpu.VMEM((MODES, 64), BF16),
            pltpu.VMEM((MODES, FAMILIES * MODES), BF16),
            pltpu.VMEM((32, 2 * MODES), BF16),
            pltpu.VMEM((7,) + shape, F32),
            field,
        ]
        + [field] * 10
        + [
            pltpu.SemaphoreType.DMA((N_EX, 5)),
            pltpu.SemaphoreType.DMA((N_EX, 5)),
            pltpu.SemaphoreType.DMA((N_RED, 32)),
            pltpu.SemaphoreType.DMA((N_RED, 32)),
            pltpu.SemaphoreType.DMA((N_IN,)),
        ],
        compiler_params=pltpu.CompilerParams(
            collective_id=0, has_side_effects=True, vmem_limit_bytes=60 * 1024 * 1024
        ),
        name="newton_step",
    )(displacement, load_field, foundation, flags, slots, family_in, family_mid, family_out, family_tan)
    return displacement + gain, residual - change


def solution(mesh):
    placed = P("blk", "micro", "slab")
    return jax.shard_map(
        body,
        mesh=mesh,
        in_specs=(placed,) * 5 + (P(),) * 4,
        out_specs=(placed, placed),
        check_vma=False,
    )
```

```python
import jax
import jax.numpy as jnp
from jax import lax
from jax.experimental import pallas as pl
from jax.experimental.pallas import tpu as pltpu
from jax.sharding import PartitionSpec as P

F32 = jnp.float32
BF16 = jnp.bfloat16
MESH = pl.DeviceIdType.MESH
FAMILIES = 4
MODES = 256
CAP_SHIFT = 14
SIGMA = 3.0
NX, NY, NZ = 8, 32, 128
TILES = NY // 8
E_DISP, E_TAN, E_SX, E_SY, E_R, E_W, E_T = 0, 1, 2, 3, 4, 5, 6
N_EX = 12
INSIDE = (2, 3, 4, 5)
OUTSIDE = (0, 1, 6, 7)
N_RED = 4
N_IN = 12
FIX = NX * NY * 8
N_DOT = 13


def prepare_weights(family_in, family_out, family_tan, w_in, w_out):
    zero = jnp.zeros((1, MODES), F32)
    high, low, stress, tangent = [], [], [], []
    for f in range(FAMILIES):
        weight = family_in[:, f, :]
        rounded = weight.astype(BF16).astype(F32)
        high += [rounded, rounded, zero, zero]
        low += [weight - rounded, zero, zero, zero, zero, zero]
        tan = family_tan[f : f + 1, :]
        tan_high = tan.astype(BF16).astype(F32)
        stress += [family_out[:, f, :].astype(F32)] + [zero] * 5
        tangent += [zero] * 3 + [tan_high, tan - tan_high] + [zero] * 3
    w_in[...] = jnp.concatenate(high + low, axis=0).T.astype(BF16)
    w_out[:, :MODES] = jnp.concatenate(stress, axis=0).astype(BF16)
    w_out[:, MODES:] = jnp.concatenate(tangent, axis=0).astype(BF16)


def fibre_chunk(points, w_in, w_mid, w_out, places):
    width = len(places) * NZ
    rows = jnp.concatenate([points[pl.ds(place, 8), :] for place in places], axis=1)
    family, flag = rows[6:7, :], rows[7:8, :]
    family_8 = jnp.broadcast_to(family, (8, width))
    chosen = [family_8 == float(f) for f in range(FAMILIES)]
    strain = jnp.concatenate([jnp.where(m, rows, 0.0) for m in chosen], axis=0).astype(BF16)
    modal = jnp.dot(w_in[...], jnp.concatenate([strain, strain], axis=0), preferred_element_type=F32)
    modal = modal.reshape(MODES // 8, 8, width)
    plastic = jnp.broadcast_to(flag, (8, width)) > 0.5
    active = jnp.where(plastic[None], jnp.tanh(modal), modal).reshape(MODES, width).astype(BF16)
    active = active.reshape(MODES // 16, 16, width)
    family_16 = jnp.broadcast_to(family, (16, width))
    parts = []
    for f in range(FAMILIES):
        mask = jnp.where(family_16 == float(f), 1.0, 0.0).astype(BF16)
        parts.append((active * mask[None]).reshape(MODES, width))
    hidden = jnp.dot(w_mid[...], jnp.concatenate(parts, axis=0), preferred_element_type=F32)
    bounded = jnp.tanh(hidden).astype(BF16)
    out = jnp.dot(
        w_out[...], jnp.concatenate([bounded, bounded * bounded], axis=0), preferred_element_type=F32
    )
    picked = jnp.where(
        chosen[0], out[0:8], jnp.where(chosen[1], out[8:16], jnp.where(chosen[2], out[16:24], out[24:32]))
    )
    for i, place in enumerate(places):
        points[pl.ds(place, 8), :] = picked[:, i * NZ : (i + 1) * NZ]


def newton_kernel(
    disp_hbm, load_hbm, found_hbm, flags_hbm, slot_hbm, fin_hbm, fmid_hbm, fout_hbm, ftan_hbm,
    gain_out, residual_out, change_out,
    load_ref, found_ref, flags_ref, slot_ref, fin_ref, fout_ref, ftan_ref,
    ex, zsend, zrecv, red, points, w_in, w_mid, w_out, coef, s_z,
    x_, r_, w_, z_, z2_, p_, s_, t_, u_, v_,
    send_sem, recv_sem, red_send, red_recv, in_sem,
):
    inner = pl.ds(8, NY)
    pairs = [(disp_hbm, ex.at[E_DISP, pl.ds(2, NX), inner, :]), (slot_hbm, slot_ref), (flags_hbm, flags_ref)]
    pairs += [(fin_hbm, fin_ref), (fout_hbm, fout_ref), (ftan_hbm, ftan_ref)]
    pairs += [(fmid_hbm.at[f], w_mid.at[:, pl.ds(f * MODES, MODES)]) for f in range(FAMILIES)]
    pairs += [(found_hbm, found_ref), (load_hbm, load_ref)]
    loads = [pltpu.make_async_copy(a, b, in_sem.at[j]) for j, (a, b) in enumerate(pairs)]
    for c in loads:
        c.start()
    blk, slab, micro = lax.axis_index("blk"), lax.axis_index("slab"), lax.axis_index("micro")
    n_blk = lax.axis_size("blk")
    up_blk, down_blk = lax.rem(blk + 1, n_blk), lax.rem(blk + n_blk - 1, n_blk)
    part_x = slab * 4 + micro

    def peer_x(step):
        other = lax.rem(part_x + step, 8)
        return (blk, lax.div(other, 4), lax.rem(other, 4))

    def peer_blk(step):
        return (lax.rem(blk + step, n_blk), slab, micro)

    barrier = pltpu.get_barrier_semaphore()
    friends = [peer_x(j) for j in range(1, 8)] + [peer_blk(j) for j in range(1, 16)]
    for friend in friends:
        pl.semaphore_signal(barrier, inc=1, device_id=friend, device_id_type=MESH)

    lane = lax.broadcasted_iota(jnp.int32, (8, NZ), 1)
    diagonal = lax.broadcasted_iota(jnp.int32, (16, NZ), 0) == lax.broadcasted_iota(jnp.int32, (16, NZ), 1)
    first_slab, last_slab = slab == 0, slab == 1
    pack_id = {n: lax.div(lax.rem(lane + n * (1 - slab), NZ), n) for n in (1, 2)}
    edge_own = jnp.logical_or(jnp.logical_and(lane == NZ - 1, slab == 0), jnp.logical_and(lane == 0, slab == 1))
    edge_up = {n: jnp.logical_and(lane < n, first_slab) for n in (1, 2)}
    edge_down = {n: jnp.logical_and(lane >= NZ - n, last_slab) for n in (1, 2)}

    def keep(condition):
        return jnp.where(condition, 0.0, 1.0).astype(F32)

    keep_up_1 = keep(jnp.logical_and(lane == NZ - 1, last_slab))[None]
    keep_down_1 = keep(jnp.logical_and(lane == 0, first_slab))[None]
    keep_up_2 = keep(jnp.logical_and(lane >= NZ - 2, last_slab))[None]
    keep_down_2 = keep(jnp.logical_and(lane < 2, first_slab))[None]

    @pl.when(micro == 0)
    def _():
        for e in range(N_EX):
            ex[e, :, 0:8, :] = jnp.zeros((NX + 4, 8, NZ), F32)

    @pl.when(micro == 3)
    def _():
        for e in range(N_EX):
            ex[e, :, NY + 8 : NY + 16, :] = jnp.zeros((NX + 4, 8, NZ), F32)

    def copy(source, target, e, k, device):
        return pltpu.make_async_remote_copy(
            src_ref=source, dst_ref=target, send_sem=send_sem.at[e, k], recv_sem=recv_sem.at[e, k],
            device_id=device, device_id_type=MESH,
        )

    def copies_x(e, depth):
        up = copy(
            ex.at[e, pl.ds(NX + 2 - depth, depth), pl.ds(8, NY), :],
            ex.at[e, pl.ds(2 - depth, depth), pl.ds(8, NY), :], e, 0, (up_blk, slab, micro),
        )
        down = copy(
            ex.at[e, pl.ds(2, depth), pl.ds(8, NY), :],
            ex.at[e, pl.ds(NX + 2, depth), pl.ds(8, NY), :], e, 1, (down_blk, slab, micro),
        )
        return up, down

    def copies_y(e):
        up = copy(
            ex.at[e, pl.ds(2, NX), pl.ds(NY, 8), :], ex.at[e, pl.ds(2, NX), pl.ds(0, 8), :],
            e, 2, (blk, slab, lax.rem(micro + 1, 4)),
        )
        down = copy(
            ex.at[e, pl.ds(2, NX), pl.ds(8, 8), :], ex.at[e, pl.ds(2, NX), pl.ds(NY + 8, 8), :],
            e, 3, (blk, slab, lax.rem(micro + 3, 4)),
        )
        return up, down

    def copy_z(e):
        return copy(zsend.at[e], zrecv.at[e], e, 4, (blk, 1 - slab, micro))

    def start(e, depth, x=True, y=True, z=True):
        if x:
            for c in copies_x(e, depth):
                c.start()
        if z:
            copy_z(e).start()
        if y:
            up, down = copies_y(e)

            @pl.when(micro < 3)
            def _():
                up.start()

            @pl.when(micro > 0)
            def _():
                down.start()

    def finish(e, depth, x=True, y=True, z=True):
        if x:
            for c in copies_x(e, depth):
                c.wait_recv()
        if z:
            copy_z(e).wait_recv()
        if y:
            up, down = copies_y(e)

            @pl.when(micro > 0)
            def _():
                up.wait_recv()

            @pl.when(micro < 3)
            def _():
                down.wait_recv()

    def drain(e, depth, x=True, y=True, z=True):
        if x:
            for c in copies_x(e, depth):
                c.wait_send()
        if z:
            copy_z(e).wait_send()
        if y:
            up, down = copies_y(e)

            @pl.when(micro < 3)
            def _():
                up.wait_send()

            @pl.when(micro > 0)
            def _():
                down.wait_send()

    def pack_plane(packed, plane, i, step=2):
        for q in range(TILES):
            n = i * TILES + q
            tile = plane[8 * q : 8 * q + 8]
            packed = jnp.where(pack_id[step] == n, pltpu.roll(tile, step * n, 1) if n else tile, packed)
        return packed

    def shifted_z(plane, message, i, step):
        tiles_up, tiles_down = [], []
        for q in range(TILES):
            n = i * TILES + q
            tile = plane[8 * q : 8 * q + 8]
            halo = pltpu.roll(message, NZ - step * n, 1) if n else message
            tiles_up.append(pltpu.roll(jnp.where(edge_up[step], halo, tile), NZ - step, 1))
            tiles_down.append(pltpu.roll(jnp.where(edge_down[step], halo, tile), step, 1))
        return jnp.concatenate(tiles_up, axis=0), jnp.concatenate(tiles_down, axis=0)

    def masked(plane, mask):
        return (plane.reshape(-1, 8, NZ) * mask).reshape(plane.shape)

    def put(e, i, plane):
        ex[e, 2 + i, inner, :] = plane

    def operator(e, planes, write):
        message = zrecv[e]
        for i in planes:
            value = ex[e, 2 + i, inner, :]
            z_up, z_down = shifted_z(value, message, i, 2)
            total = coef[0, i] * value
            total -= coef[1, i] * ex[e, 4 + i, inner, :] + coef[2, i] * ex[e, i, inner, :]
            total -= coef[3, i] * ex[e, 2 + i, 10 : 10 + NY, :] + coef[4, i] * ex[e, 2 + i, 6 : 6 + NY, :]
            total -= coef[5, i] * z_up + coef[6, i] * z_down
            write(i, total)

    def red_copy(k, stage, step, peer, mine):
        n = stage * 16 + step
        return pltpu.make_async_remote_copy(
            src_ref=red.at[k, stage, mine], dst_ref=red.at[k, stage, mine],
            send_sem=red_send.at[k, n], recv_sem=red_recv.at[k, n], device_id=peer, device_id_type=MESH,
        )

    stages = ((peer_x, part_x, 8), (peer_blk, blk, 16))

    def red_start(k, stage, rows):
        peer, mine, count = stages[stage]
        red[k, stage, mine] = rows
        for step in range(1, count):
            red_copy(k, stage, step, peer(step), mine).start()

    def red_finish(k, stage):
        peer, mine, count = stages[stage]
        for step in range(1, count):
            red_copy(k, stage, step, peer(step), mine).wait_recv()
        total = red[k, stage, 0]
        for j in range(1, count):
            total = total + red[k, stage, j]
        return total

    def red_drain(k):
        for stage, (peer, mine, count) in enumerate(stages):
            for step in range(1, count):
                red_copy(k, stage, step, peer(step), mine).wait_send()

    def add_dots(sums, r, w, p, s, t):
        kp = s + SIGMA * p
        kr = w + SIGMA * r
        kkp = (t + SIGMA * s) + SIGMA * kp
        terms = (
            r * r, r * kp, r * kr, r * kkp, kp * kp, kp * kr, kp * kkp,
            kr * kr, kr * kkp, kkp * kkp, p * kp, p * kr, p * kkp,
        )
        folded = [term.reshape(TILES, 8, NZ).sum(axis=0) for term in terms]
        return folded if sums is None else [a + b for a, b in zip(sums, folded)]

    def row_of(sums):
        rows = [jnp.sum(a, axis=0, keepdims=True) for a in sums]
        rows = jnp.concatenate(rows + [jnp.zeros((16 - N_DOT, NZ), F32)], axis=0)
        sums = jnp.broadcast_to(jnp.sum(rows, axis=1, keepdims=True), (16, NZ))
        return jnp.sum(jnp.where(diagonal, sums, 0.0), axis=0, keepdims=True)

    def scalars(rows):
        d = jnp.sum(jnp.where(diagonal, jnp.broadcast_to(rows, (16, NZ)), 0.0), axis=1, keepdims=True)
        g = [d[j : j + 1, :] for j in range(N_DOT)]
        rr, rs, rw, rt, ss, sw, st, ww, wt, tt, ps, pw, pt = g
        alpha = rr / ps
        rr_1 = rr - 2.0 * alpha * rs + alpha * alpha * ss
        beta_1 = rr_1 / rr
        r_q = rw - alpha * rt + beta_1 * rs
        s_q = sw - alpha * st + beta_1 * ss
        p_q = pw - alpha * pt + beta_1 * ps
        alpha_1 = rr_1 / (r_q - alpha * s_q + beta_1 * p_q)
        w_q = ww - alpha * wt + beta_1 * sw
        t_q = wt - alpha * tt + beta_1 * st
        q_q = w_q - alpha * t_q + beta_1 * s_q
        rr_2 = rr_1 - 2.0 * alpha_1 * (r_q - alpha * s_q) + alpha_1 * alpha_1 * q_q
        beta_2 = rr_2 / rr_1
        return [jnp.broadcast_to(a, (NY, NZ)) for a in (alpha, beta_1, alpha_1, beta_2)]

    zeros = jnp.zeros((8, NZ), F32)

    def strains_at(i, halo):
        value = ex[E_DISP, 2 + i, inner, :]
        if halo is None:
            y_up, y_down = pltpu.roll(value, NY - 1, 0), pltpu.roll(value, 1, 0)
            z_up, z_down = pltpu.roll(value, NZ - 1, 1), pltpu.roll(value, 1, 1)
        else:
            y_up, y_down = ex[E_DISP, 2 + i, 9 : 9 + NY, :], ex[E_DISP, 2 + i, 7 : 7 + NY, :]
            z_up, z_down = shifted_z(value, halo, i, 1)
        return (
            (ex[E_DISP, 3 + i, inner, :] - ex[E_DISP, 1 + i, inner, :]) * 0.5,
            (y_up - y_down) * 0.5,
            (masked(z_up, keep_up_1) - masked(z_down, keep_down_1)) * 0.5,
        )

    def store_points(base, count, strains, family, flag):
        rounded = [s.astype(BF16).astype(F32) for s in strains]
        rows = rounded + [s - h for s, h in zip(strains, rounded)] + [family, flag]
        for k, row in enumerate(rows):
            points[pl.ds(base + k, count, stride=8), :] = row

    def traits(i):
        family = lax.shift_right_logical(slot_ref[i], CAP_SHIFT).astype(F32)
        return family, flags_ref[i].astype(F32)

    def chunks(first, last, size, start_of):
        def chunk(j, carry):
            fibre_chunk(points, w_in, w_mid, w_out, [start_of(j * size + i) for i in range(size)])
            return carry

        lax.fori_loop(first, last, chunk, 0)

    def inner_row(m):
        plane = lax.div(m, NY - 2) + 1
        return pl.multiple_of((plane * NY + lax.rem(m, NY - 2) + 1) * 8, 8)

    def face_row(m):
        return pl.multiple_of((m + lax.div(m, NY) * ((NX - 2) * NY)) * 8, 8)

    middle = range(1, NX - 1)
    loads[0].wait()
    packed = zeros
    for i in range(NX):
        packed = pack_plane(packed, ex[E_DISP, 2 + i, inner, :], i, 1)
    zsend[E_DISP] = packed
    for c in loads[1:10]:
        c.wait()
    prepare_weights(fin_ref, fout_ref, ftan_ref, w_in, w_out)
    for i in middle:
        store_points(i * NY * 8, NY, strains_at(i, None), *traits(i))

    chunks(0, 1, 32, inner_row)
    pl.semaphore_wait(barrier, len(friends))
    start(E_DISP, 1)
    chunks(1, 3, 32, inner_row)
    finish(E_DISP, 1)
    message = zrecv[E_DISP]
    edges = [zeros] * 5
    for i in range(NX):
        columns = strains_at(i, message) + traits(i)
        edges = [pack_plane(e, c, i, 1) for e, c in zip(edges, columns)]
        if i in middle:
            for y in (0, NY - 1):
                part = [c[y : y + 1] for c in columns]
                store_points((i * NY + y) * 8, 1, part[:3], part[3], part[4])
        else:
            store_points(i * NY * 8, NY, columns[:3], columns[3], columns[4])
    store_points(FIX, 8, edges[:3], edges[3], edges[4])
    sides = [(i * NY + y) * 8 for i in middle for y in (0, NY - 1)]
    rest = [((NX - 2) * NY + y) * 8 for y in range(NY - 5, NY - 1)]
    fibre_chunk(points, w_in, w_mid, w_out, [FIX + 8 * i for i in range(8)] + sides + rest)
    chunks(0, 2, 32, face_row)

    def results(base, count):
        sx, sy, sz, high, low = [points[pl.ds(base + k, count, stride=8), :] for k in range(5)]
        return sx, sy, sz, 0.5 + (high + low)

    def keep_results(i, top, count, values):
        rows = pl.ds(8 + top, count)
        ex[E_SX, 2 + i, rows, :] = values[0]
        ex[E_SY, 2 + i, rows, :] = values[1]
        s_z[i, pl.ds(top, count), :] = values[2]
        ex[E_TAN, 2 + i, rows, :] = values[3]

    edges = results(FIX, 8)
    zsend[E_SX] = edges[2]
    zsend[E_TAN] = edges[3]
    for i in range(NX):
        if i in middle:
            for y in (0, NY - 1):
                keep_results(i, y, 1, results((i * NY + y) * 8, 1))
        else:
            keep_results(i, 0, NY, results(i * NY * 8, NY))
    start(E_SX, 1, y=False)
    start(E_TAN, 1)
    start(E_SY, 1, x=False, z=False)
    chunks(0, 2, 40, lambda m: inner_row(m + 96))
    drain(E_TAN, 1, x=False, z=False)
    drain(E_SY, 1, x=False, z=False)
    for i in middle:
        values = results(i * NY * 8, NY)
        columns = []
        for e, v in zip(edges, values):
            tiles = [
                jnp.where(edge_own, pltpu.roll(e, NZ - (i * TILES + q), 1), v[8 * q : 8 * q + 8])
                for q in range(TILES)
            ]
            columns.append(jnp.concatenate(tiles, axis=0))
        keep_results(i, 0, NY, columns)

    loads[10].wait()
    loads[11].wait()
    finish(E_SX, 1, y=False)
    finish(E_TAN, 1)
    finish(E_SY, 1, x=False, z=False)
    message_s, message_t = zrecv[E_SX], zrecv[E_TAN]
    packed = zeros
    for i in OUTSIDE + INSIDE:
        up, down = shifted_z(s_z[i], message_s, i, 1)
        total = (ex[E_SX, 3 + i, inner, :] - ex[E_SX, 1 + i, inner, :]) * 0.5
        total += (ex[E_SY, 2 + i, 9 : 9 + NY, :] - ex[E_SY, 2 + i, 7 : 7 + NY, :]) * 0.5
        total += (masked(up, keep_up_1) - masked(down, keep_down_1)) * 0.5
        rhs = load_ref[i] - found_ref[i] * ex[E_DISP, 2 + i, inner, :] + total
        put(E_R, i, rhs)
        packed = pack_plane(packed, rhs, i)
        r_[i] = rhs
        p_[i] = rhs
        x_[i] = jnp.zeros((NY, NZ), F32)
        u_[i] = jnp.zeros((NY, NZ), F32)
        if i == OUTSIDE[-1]:
            start(E_R, 2, y=False, z=False)
    zsend[E_R] = packed
    start(E_R, 2, x=False)
    for i in range(NX):
        up, down = shifted_z(ex[E_TAN, 2 + i, inner, :], message_t, i, 1)
        z_up, z_down = masked(up, keep_up_1) * 0.25, masked(down, keep_down_1) * 0.25
        x_up, x_down = ex[E_TAN, 3 + i, inner, :] * 0.25, ex[E_TAN, 1 + i, inner, :] * 0.25
        y_up, y_down = ex[E_TAN, 2 + i, 9 : 9 + NY, :] * 0.25, ex[E_TAN, 2 + i, 7 : 7 + NY, :] * 0.25
        coef[0, i] = found_ref[i] + ((x_up + x_down) + (y_up + y_down) + (z_up + z_down)) - SIGMA
        coef[1, i], coef[2, i] = x_up, x_down
        coef[3, i], coef[4, i] = y_up, y_down
        coef[5, i], coef[6, i] = masked(z_up, keep_up_2), masked(z_down, keep_down_2)

    def step(e, target, write, between=lambda: None):
        box = [zeros]

        def store(i, value):
            put(target, i, value)
            write(i, value)
            box[0] = pack_plane(box[0], value, i)

        finish(e, 2, x=False)
        operator(e, INSIDE, store)
        between()
        finish(e, 2, y=False, z=False)
        operator(e, OUTSIDE, store)
        start(target, 2, y=False, z=False)
        zsend[target] = box[0]
        start(target, 2, x=False)

    def write_w(i, value):
        w_[i] = value
        s_[i] = value

    def write_z(i, value):
        z_[i] = value
        t_[i] = value

    step(E_R, E_W, write_w)
    step(E_W, E_T, write_z)
    sums = None
    for i in range(NX):
        sums = add_dots(sums, r_[i], w_[i], p_[i], s_[i], t_[i])
    red_start(0, 0, row_of(sums))

    def block(k, beta):
        e_t, e_u = E_T + 2 * k, E_T + 2 * k + 1

        def write_u(i, value):
            z2_[i] = value - beta * u_[i]
            u_[i] = value

        step(e_t, e_u, write_u, lambda: red_start(k, 1, red_finish(k, 0)))

        def write_v(i, value):
            v_[i] = value

        finish(e_u, 2, x=False)
        operator(e_u, INSIDE, write_v)
        alpha, beta_1, alpha_1, beta_2 = scalars(red_finish(k, 1))
        box = [zeros]
        sums = None

        def update(i):
            p, s, t, u = p_[i], s_[i], t_[i], u_[i]
            x = x_[i] + alpha * p
            r = r_[i] - alpha * (s + SIGMA * p)
            w = w_[i] - alpha * (t + SIGMA * s)
            z = z_[i] - alpha * (u + SIGMA * t)
            z2 = z2_[i] - alpha * (v_[i] + SIGMA * u)
            p = r + beta_1 * p
            s = w + beta_1 * s
            t = z + beta_1 * t
            u = z2 + beta_1 * u
            x_[i] = x + alpha_1 * p
            r = r - alpha_1 * (s + SIGMA * p)
            w = w - alpha_1 * (t + SIGMA * s)
            z = z - alpha_1 * (u + SIGMA * t)
            r_[i], w_[i], z_[i], u_[i] = r, w, z, u
            p = r + beta_2 * p
            s = w + beta_2 * s
            t = z + beta_2 * t
            p_[i], s_[i], t_[i] = p, s, t
            put(e_t + 2, i, t)
            box[0] = pack_plane(box[0], t, i)

        for i in INSIDE:
            update(i)
            sums = add_dots(sums, r_[i], w_[i], p_[i], s_[i], t_[i])
        finish(e_u, 2, y=False, z=False)
        operator(e_u, OUTSIDE, write_v)
        for i in OUTSIDE:
            update(i)

        @pl.when(k < 2)
        def _():
            start(e_t + 2, 2, y=False, z=False)
            zsend[e_t + 2] = box[0]
            start(e_t + 2, 2, x=False)

        for i in OUTSIDE:
            sums = add_dots(sums, r_[i], w_[i], p_[i], s_[i], t_[i])
        red_start(k + 1, 0, row_of(sums))
        return beta_2

    lax.fori_loop(0, 3, block, jnp.zeros((NY, NZ), F32))

    last = N_RED - 1
    red_start(last, 1, red_finish(last, 0))
    alpha, beta_1, alpha_1, _ = scalars(red_finish(last, 1))
    for i in range(NX):
        p, s, t = p_[i], s_[i], t_[i]
        x = x_[i] + alpha * p
        r = r_[i] - alpha * (s + SIGMA * p)
        w = w_[i] - alpha * (t + SIGMA * s)
        p = r + beta_1 * p
        s = w + beta_1 * s
        gain_out[i] = x + alpha_1 * p
        residual_out[i] = r
        change_out[i] = alpha_1 * (s + SIGMA * p)

    drain(E_DISP, 1)
    drain(E_SX, 1, y=False)
    drain(E_TAN, 1, y=False)

    def drain_step(e, carry):
        drain(e, 2)
        return carry

    lax.fori_loop(E_R, N_EX, drain_step, 0)

    def drain_red(k, carry):
        red_drain(k)
        return carry

    lax.fori_loop(0, N_RED, drain_red, 0)


def body(displacement, load_field, foundation, flags, slots, family_in, family_mid, family_out, family_tan):
    family_in, family_out = jnp.transpose(family_in, (1, 0, 2)), jnp.transpose(family_out, (1, 0, 2))
    shape = (NX, NY, NZ)
    field = pltpu.VMEM(shape, F32)
    ints = pltpu.VMEM(shape, jnp.int32)
    whole = pl.BlockSpec(memory_space=pltpu.VMEM)
    gain, residual, change = pl.pallas_call(
        newton_kernel,
        out_shape=(jax.ShapeDtypeStruct(shape, F32),) * 3,
        in_specs=[pl.BlockSpec(memory_space=pl.ANY)] * 9,
        out_specs=(whole,) * 3,
        scratch_shapes=[
            field,
            field,
            ints,
            ints,
            pltpu.VMEM((3, FAMILIES, MODES), F32),
            pltpu.VMEM((3, FAMILIES, MODES), BF16),
            pltpu.VMEM((FAMILIES, MODES), F32),
            pltpu.VMEM((N_EX + 1, NX + 4, NY + 16, NZ), F32),
            pltpu.VMEM((N_EX, 8, NZ), F32),
            pltpu.VMEM((N_EX, 8, NZ), F32),
            pltpu.VMEM((N_RED, 2, 16, 1, NZ), F32),
            pltpu.VMEM((FIX + 64, NZ), F32),
            pltpu.VMEM((MODES, 64), BF16),
            pltpu.VMEM((MODES, FAMILIES * MODES), BF16),
            pltpu.VMEM((32, 2 * MODES), BF16),
            pltpu.VMEM((7,) + shape, F32),
            field,
        ]
        + [field] * 10
        + [
            pltpu.SemaphoreType.DMA((N_EX, 5)),
            pltpu.SemaphoreType.DMA((N_EX, 5)),
            pltpu.SemaphoreType.DMA((N_RED, 32)),
            pltpu.SemaphoreType.DMA((N_RED, 32)),
            pltpu.SemaphoreType.DMA((N_IN,)),
        ],
        compiler_params=pltpu.CompilerParams(
            collective_id=0, has_side_effects=True, vmem_limit_bytes=60 * 1024 * 1024
        ),
        name="newton_step",
    )(displacement, load_field, foundation, flags, slots, family_in, family_mid, family_out, family_tan)
    return displacement + gain, residual - change


def solution(mesh):
    placed = P("blk", "micro", "slab")
    return jax.shard_map(
        body,
        mesh=mesh,
        in_specs=(placed,) * 5 + (P(),) * 4,
        out_specs=(placed, placed),
        check_vma=False,
    )
```

```python
import jax
import jax.numpy as jnp
from jax import lax
from jax.experimental import pallas as pl
from jax.experimental.pallas import tpu as pltpu
from jax.sharding import PartitionSpec as P

F32 = jnp.float32
BF16 = jnp.bfloat16
MESH = pl.DeviceIdType.MESH
FAMILIES = 4
MODES = 256
CAP_SHIFT = 14
SIGMA = 3.0
NX, NY, NZ = 8, 32, 128
TILES = NY // 8
E_DISP, E_TAN, E_SX, E_SY, E_R, E_W, E_T = 0, 1, 2, 3, 4, 5, 6
N_EX = 12
INSIDE = (2, 3, 4, 5)
OUTSIDE = (0, 1, 6, 7)
N_RED = 4
N_IN = 12
FIX = NX * NY * 8
N_DOT = 13


def prepare_weights(family_in, family_out, family_tan, w_in, w_out):
    zero = jnp.zeros((1, MODES), F32)
    high, low, stress, tangent = [], [], [], []
    for f in range(FAMILIES):
        weight = family_in[:, f, :]
        rounded = weight.astype(BF16).astype(F32)
        high += [rounded, rounded, zero, zero]
        low += [weight - rounded, zero, zero, zero, zero, zero]
        tan = family_tan[f : f + 1, :]
        tan_high = tan.astype(BF16).astype(F32)
        stress += [family_out[:, f, :].astype(F32)] + [zero] * 5
        tangent += [zero] * 3 + [tan_high, tan - tan_high] + [zero] * 3
    w_in[...] = jnp.concatenate(high + low, axis=0).T.astype(BF16)
    w_out[:, :MODES] = jnp.concatenate(stress, axis=0).astype(BF16)
    w_out[:, MODES:] = jnp.concatenate(tangent, axis=0).astype(BF16)


def fibre_chunk(points, w_in, w_mid, w_out, places):
    width = len(places) * NZ
    rows = jnp.concatenate([points[pl.ds(place, 8), :] for place in places], axis=1)
    family, flag = rows[6:7, :], rows[7:8, :]
    family_8 = jnp.broadcast_to(family, (8, width))
    chosen = [family_8 == float(f) for f in range(FAMILIES)]
    strain = jnp.concatenate([jnp.where(m, rows, 0.0) for m in chosen], axis=0).astype(BF16)
    modal = jnp.dot(w_in[...], jnp.concatenate([strain, strain], axis=0), preferred_element_type=F32)
    modal = modal.reshape(MODES // 8, 8, width)
    plastic = jnp.broadcast_to(flag, (8, width)) > 0.5
    active = jnp.where(plastic[None], jnp.tanh(modal), modal).reshape(MODES, width).astype(BF16)
    active = active.reshape(MODES // 16, 16, width)
    family_16 = jnp.broadcast_to(family, (16, width))
    parts = []
    for f in range(FAMILIES):
        mask = jnp.where(family_16 == float(f), 1.0, 0.0).astype(BF16)
        parts.append((active * mask[None]).reshape(MODES, width))
    hidden = jnp.dot(w_mid[...], jnp.concatenate(parts, axis=0), preferred_element_type=F32)
    bounded = jnp.tanh(hidden).astype(BF16)
    out = jnp.dot(
        w_out[...], jnp.concatenate([bounded, bounded * bounded], axis=0), preferred_element_type=F32
    )
    picked = jnp.where(
        chosen[0], out[0:8], jnp.where(chosen[1], out[8:16], jnp.where(chosen[2], out[16:24], out[24:32]))
    )
    for i, place in enumerate(places):
        points[pl.ds(place, 8), :] = picked[:, i * NZ : (i + 1) * NZ]


def newton_kernel(
    disp_hbm, load_hbm, found_hbm, flags_hbm, slot_hbm, fin_hbm, fmid_hbm, fout_hbm, ftan_hbm,
    field_out, residual_out, change_out,
    load_ref, found_ref, flags_ref, slot_ref, fin_ref, fout_ref, ftan_ref,
    ex, zsend, zrecv, red, points, w_in, w_mid, w_out, coef, s_z,
    x_, r_, w_, z_, z2_, p_, s_, t_, u_, v_,
    send_sem, recv_sem, red_send, red_recv, in_sem,
):
    inner = pl.ds(8, NY)
    pairs = [(disp_hbm, ex.at[E_DISP, pl.ds(2, NX), inner, :]), (slot_hbm, slot_ref), (flags_hbm, flags_ref)]
    pairs += [(fin_hbm, fin_ref), (fout_hbm, fout_ref), (ftan_hbm, ftan_ref)]
    pairs += [(fmid_hbm.at[f], w_mid.at[:, pl.ds(f * MODES, MODES)]) for f in range(FAMILIES)]
    pairs += [(found_hbm, found_ref), (load_hbm, load_ref)]
    loads = [pltpu.make_async_copy(a, b, in_sem.at[j]) for j, (a, b) in enumerate(pairs)]
    for c in loads:
        c.start()
    blk, slab, micro = lax.axis_index("blk"), lax.axis_index("slab"), lax.axis_index("micro")
    n_blk = lax.axis_size("blk")
    up_blk, down_blk = lax.rem(blk + 1, n_blk), lax.rem(blk + n_blk - 1, n_blk)
    part_x = slab * 4 + micro

    def peer_x(step):
        other = lax.rem(part_x + step, 8)
        return (blk, lax.div(other, 4), lax.rem(other, 4))

    def peer_blk(step):
        return (lax.rem(blk + step, n_blk), slab, micro)

    barrier = pltpu.get_barrier_semaphore()
    friends = [peer_x(j) for j in range(1, 8)] + [peer_blk(j) for j in range(1, 16)]
    for friend in friends:
        pl.semaphore_signal(barrier, inc=1, device_id=friend, device_id_type=MESH)

    lane = lax.broadcasted_iota(jnp.int32, (8, NZ), 1)
    diagonal = lax.broadcasted_iota(jnp.int32, (16, NZ), 0) == lax.broadcasted_iota(jnp.int32, (16, NZ), 1)
    first_slab, last_slab = slab == 0, slab == 1
    pack_id = {n: lax.div(lax.rem(lane + n * (1 - slab), NZ), n) for n in (1, 2)}
    edge_own = jnp.logical_or(jnp.logical_and(lane == NZ - 1, slab == 0), jnp.logical_and(lane == 0, slab == 1))
    edge_up = {n: jnp.logical_and(lane < n, first_slab) for n in (1, 2)}
    edge_down = {n: jnp.logical_and(lane >= NZ - n, last_slab) for n in (1, 2)}

    def keep(condition):
        return jnp.where(condition, 0.0, 1.0).astype(F32)

    keep_up_1 = keep(jnp.logical_and(lane == NZ - 1, last_slab))[None]
    keep_down_1 = keep(jnp.logical_and(lane == 0, first_slab))[None]
    keep_up_2 = keep(jnp.logical_and(lane >= NZ - 2, last_slab))[None]
    keep_down_2 = keep(jnp.logical_and(lane < 2, first_slab))[None]

    @pl.when(micro == 0)
    def _():
        for e in range(N_EX):
            ex[e, :, 0:8, :] = jnp.zeros((NX + 4, 8, NZ), F32)

    @pl.when(micro == 3)
    def _():
        for e in range(N_EX):
            ex[e, :, NY + 8 : NY + 16, :] = jnp.zeros((NX + 4, 8, NZ), F32)

    def copy(source, target, e, k, device):
        return pltpu.make_async_remote_copy(
            src_ref=source, dst_ref=target, send_sem=send_sem.at[e, k], recv_sem=recv_sem.at[e, k],
            device_id=device, device_id_type=MESH,
        )

    def copies_x(e, depth):
        up = copy(
            ex.at[e, pl.ds(NX + 2 - depth, depth), pl.ds(8, NY), :],
            ex.at[e, pl.ds(2 - depth, depth), pl.ds(8, NY), :], e, 0, (up_blk, slab, micro),
        )
        down = copy(
            ex.at[e, pl.ds(2, depth), pl.ds(8, NY), :],
            ex.at[e, pl.ds(NX + 2, depth), pl.ds(8, NY), :], e, 1, (down_blk, slab, micro),
        )
        return up, down

    def copies_y(e):
        up = copy(
            ex.at[e, pl.ds(2, NX), pl.ds(NY, 8), :], ex.at[e, pl.ds(2, NX), pl.ds(0, 8), :],
            e, 2, (blk, slab, lax.rem(micro + 1, 4)),
        )
        down = copy(
            ex.at[e, pl.ds(2, NX), pl.ds(8, 8), :], ex.at[e, pl.ds(2, NX), pl.ds(NY + 8, 8), :],
            e, 3, (blk, slab, lax.rem(micro + 3, 4)),
        )
        return up, down

    def copy_z(e):
        return copy(zsend.at[e], zrecv.at[e], e, 4, (blk, 1 - slab, micro))

    def start(e, depth, x=True, y=True, z=True):
        if x:
            for c in copies_x(e, depth):
                c.start()
        if z:
            copy_z(e).start()
        if y:
            up, down = copies_y(e)

            @pl.when(micro < 3)
            def _():
                up.start()

            @pl.when(micro > 0)
            def _():
                down.start()

    def finish(e, depth, x=True, y=True, z=True):
        if x:
            for c in copies_x(e, depth):
                c.wait_recv()
        if z:
            copy_z(e).wait_recv()
        if y:
            up, down = copies_y(e)

            @pl.when(micro > 0)
            def _():
                up.wait_recv()

            @pl.when(micro < 3)
            def _():
                down.wait_recv()

    def drain(e, depth, x=True, y=True, z=True):
        if x:
            for c in copies_x(e, depth):
                c.wait_send()
        if z:
            copy_z(e).wait_send()
        if y:
            up, down = copies_y(e)

            @pl.when(micro < 3)
            def _():
                up.wait_send()

            @pl.when(micro > 0)
            def _():
                down.wait_send()

    def pack_plane(packed, plane, i, step=2):
        for q in range(TILES):
            n = i * TILES + q
            tile = plane[8 * q : 8 * q + 8]
            packed = jnp.where(pack_id[step] == n, pltpu.roll(tile, step * n, 1) if n else tile, packed)
        return packed

    def shifted_z(plane, message, i, step):
        tiles_up, tiles_down = [], []
        for q in range(TILES):
            n = i * TILES + q
            tile = plane[8 * q : 8 * q + 8]
            halo = pltpu.roll(message, NZ - step * n, 1) if n else message
            tiles_up.append(pltpu.roll(jnp.where(edge_up[step], halo, tile), NZ - step, 1))
            tiles_down.append(pltpu.roll(jnp.where(edge_down[step], halo, tile), step, 1))
        return jnp.concatenate(tiles_up, axis=0), jnp.concatenate(tiles_down, axis=0)

    def masked(plane, mask):
        return (plane.reshape(-1, 8, NZ) * mask).reshape(plane.shape)

    def put(e, i, plane):
        ex[e, 2 + i, inner, :] = plane

    def operator(e, planes, write):
        message = zrecv[e]
        for i in planes:
            value = ex[e, 2 + i, inner, :]
            z_up, z_down = shifted_z(value, message, i, 2)
            total = coef[0, i] * value
            total -= coef[1, i] * ex[e, 4 + i, inner, :] + coef[2, i] * ex[e, i, inner, :]
            total -= coef[3, i] * ex[e, 2 + i, 10 : 10 + NY, :] + coef[4, i] * ex[e, 2 + i, 6 : 6 + NY, :]
            total -= coef[5, i] * z_up + coef[6, i] * z_down
            write(i, total)

    def red_copy(k, stage, step, peer, mine):
        n = stage * 16 + step
        return pltpu.make_async_remote_copy(
            src_ref=red.at[k, stage, mine], dst_ref=red.at[k, stage, mine],
            send_sem=red_send.at[k, n], recv_sem=red_recv.at[k, n], device_id=peer, device_id_type=MESH,
        )

    stages = ((peer_x, part_x, 8), (peer_blk, blk, 16))

    def red_start(k, stage, rows):
        peer, mine, count = stages[stage]
        red[k, stage, mine] = rows
        for step in range(1, count):
            red_copy(k, stage, step, peer(step), mine).start()

    def red_finish(k, stage):
        peer, mine, count = stages[stage]
        for step in range(1, count):
            red_copy(k, stage, step, peer(step), mine).wait_recv()
        total = red[k, stage, 0]
        for j in range(1, count):
            total = total + red[k, stage, j]
        return total

    def red_drain(k):
        for stage, (peer, mine, count) in enumerate(stages):
            for step in range(1, count):
                red_copy(k, stage, step, peer(step), mine).wait_send()

    def add_dots(sums, r, w, p, s, t):
        kp = s + SIGMA * p
        kr = w + SIGMA * r
        kkp = (t + SIGMA * s) + SIGMA * kp
        terms = (
            r * r, r * kp, r * kr, r * kkp, kp * kp, kp * kr, kp * kkp,
            kr * kr, kr * kkp, kkp * kkp, p * kp, p * kr, p * kkp,
        )
        folded = [term.reshape(TILES, 8, NZ).sum(axis=0) for term in terms]
        return folded if sums is None else [a + b for a, b in zip(sums, folded)]

    def row_of(sums):
        rows = [jnp.sum(a, axis=0, keepdims=True) for a in sums]
        rows = jnp.concatenate(rows + [jnp.zeros((16 - N_DOT, NZ), F32)], axis=0)
        sums = jnp.broadcast_to(jnp.sum(rows, axis=1, keepdims=True), (16, NZ))
        return jnp.sum(jnp.where(diagonal, sums, 0.0), axis=0, keepdims=True)

    def scalars(rows):
        d = jnp.sum(jnp.where(diagonal, jnp.broadcast_to(rows, (16, NZ)), 0.0), axis=1, keepdims=True)
        g = [d[j : j + 1, :] for j in range(N_DOT)]
        rr, rs, rw, rt, ss, sw, st, ww, wt, tt, ps, pw, pt = g
        alpha = rr / ps
        rr_1 = rr - 2.0 * alpha * rs + alpha * alpha * ss
        beta_1 = rr_1 / rr
        r_q = rw - alpha * rt + beta_1 * rs
        s_q = sw - alpha * st + beta_1 * ss
        p_q = pw - alpha * pt + beta_1 * ps
        alpha_1 = rr_1 / (r_q - alpha * s_q + beta_1 * p_q)
        w_q = ww - alpha * wt + beta_1 * sw
        t_q = wt - alpha * tt + beta_1 * st
        q_q = w_q - alpha * t_q + beta_1 * s_q
        rr_2 = rr_1 - 2.0 * alpha_1 * (r_q - alpha * s_q) + alpha_1 * alpha_1 * q_q
        beta_2 = rr_2 / rr_1
        return [jnp.broadcast_to(a, (NY, NZ)) for a in (alpha, beta_1, alpha_1, beta_2)]

    zeros = jnp.zeros((8, NZ), F32)

    def strains_at(i, halo):
        value = ex[E_DISP, 2 + i, inner, :]
        if halo is None:
            y_up, y_down = pltpu.roll(value, NY - 1, 0), pltpu.roll(value, 1, 0)
            z_up, z_down = pltpu.roll(value, NZ - 1, 1), pltpu.roll(value, 1, 1)
        else:
            y_up, y_down = ex[E_DISP, 2 + i, 9 : 9 + NY, :], ex[E_DISP, 2 + i, 7 : 7 + NY, :]
            z_up, z_down = shifted_z(value, halo, i, 1)
        return (
            (ex[E_DISP, 3 + i, inner, :] - ex[E_DISP, 1 + i, inner, :]) * 0.5,
            (y_up - y_down) * 0.5,
            (masked(z_up, keep_up_1) - masked(z_down, keep_down_1)) * 0.5,
        )

    def store_points(base, count, strains, family, flag):
        rounded = [s.astype(BF16).astype(F32) for s in strains]
        rows = rounded + [s - h for s, h in zip(strains, rounded)] + [family, flag]
        for k, row in enumerate(rows):
            points[pl.ds(base + k, count, stride=8), :] = row

    def traits(i):
        family = lax.shift_right_logical(slot_ref[i], CAP_SHIFT).astype(F32)
        return family, flags_ref[i].astype(F32)

    def chunks(first, last, size, start_of):
        def chunk(j, carry):
            fibre_chunk(points, w_in, w_mid, w_out, [start_of(j * size + i) for i in range(size)])
            return carry

        lax.fori_loop(first, last, chunk, 0)

    def inner_row(m):
        plane = lax.div(m, NY - 2) + 1
        return pl.multiple_of((plane * NY + lax.rem(m, NY - 2) + 1) * 8, 8)

    def face_row(m):
        return pl.multiple_of((m + lax.div(m, NY) * ((NX - 2) * NY)) * 8, 8)

    middle = range(1, NX - 1)
    loads[0].wait()
    packed = zeros
    for i in range(NX):
        packed = pack_plane(packed, ex[E_DISP, 2 + i, inner, :], i, 1)
    zsend[E_DISP] = packed
    loads[1].wait()
    loads[2].wait()
    for i in middle:
        store_points(i * NY * 8, NY, strains_at(i, None), *traits(i))
    for c in loads[3:10]:
        c.wait()
    prepare_weights(fin_ref, fout_ref, ftan_ref, w_in, w_out)

    chunks(0, 1, 32, inner_row)
    pl.semaphore_wait(barrier, len(friends))
    start(E_DISP, 1)
    chunks(1, 3, 32, inner_row)
    finish(E_DISP, 1)
    message = zrecv[E_DISP]
    edges = [zeros] * 5
    for i in range(NX):
        columns = strains_at(i, message) + traits(i)
        edges = [pack_plane(e, c, i, 1) for e, c in zip(edges, columns)]
        if i in middle:
            for y in (0, NY - 1):
                part = [c[y : y + 1] for c in columns]
                store_points((i * NY + y) * 8, 1, part[:3], part[3], part[4])
        else:
            store_points(i * NY * 8, NY, columns[:3], columns[3], columns[4])
    store_points(FIX, 8, edges[:3], edges[3], edges[4])
    sides = [(i * NY + y) * 8 for i in middle for y in (0, NY - 1)]
    rest = [((NX - 2) * NY + y) * 8 for y in range(NY - 5, NY - 1)]
    fibre_chunk(points, w_in, w_mid, w_out, [FIX + 8 * i for i in range(8)] + sides + rest)
    chunks(0, 2, 32, face_row)

    def results(base, count):
        sx, sy, sz, high, low = [points[pl.ds(base + k, count, stride=8), :] for k in range(5)]
        return sx, sy, sz, 0.5 + (high + low)

    def keep_results(i, top, count, values):
        rows = pl.ds(8 + top, count)
        ex[E_SX, 2 + i, rows, :] = values[0]
        ex[E_SY, 2 + i, rows, :] = values[1]
        s_z[i, pl.ds(top, count), :] = values[2]
        ex[E_TAN, 2 + i, rows, :] = values[3]

    edges = results(FIX, 8)
    zsend[E_SX] = edges[2]
    zsend[E_TAN] = edges[3]
    for i in range(NX):
        if i in middle:
            for y in (0, NY - 1):
                keep_results(i, y, 1, results((i * NY + y) * 8, 1))
        else:
            keep_results(i, 0, NY, results(i * NY * 8, NY))
    start(E_SX, 1, y=False)
    start(E_TAN, 1)
    start(E_SY, 1, x=False, z=False)
    chunks(0, 2, 40, lambda m: inner_row(m + 96))
    drain(E_TAN, 1, x=False, z=False)
    drain(E_SY, 1, x=False, z=False)
    for i in middle:
        values = results(i * NY * 8, NY)
        columns = []
        for e, v in zip(edges, values):
            tiles = [
                jnp.where(edge_own, pltpu.roll(e, NZ - (i * TILES + q), 1), v[8 * q : 8 * q + 8])
                for q in range(TILES)
            ]
            columns.append(jnp.concatenate(tiles, axis=0))
        keep_results(i, 0, NY, columns)

    loads[10].wait()
    loads[11].wait()
    finish(E_SX, 1, y=False)
    finish(E_TAN, 1)
    finish(E_SY, 1, x=False, z=False)
    message_s, message_t = zrecv[E_SX], zrecv[E_TAN]
    packed = zeros
    for i in OUTSIDE + INSIDE:
        up, down = shifted_z(s_z[i], message_s, i, 1)
        total = (ex[E_SX, 3 + i, inner, :] - ex[E_SX, 1 + i, inner, :]) * 0.5
        total += (ex[E_SY, 2 + i, 9 : 9 + NY, :] - ex[E_SY, 2 + i, 7 : 7 + NY, :]) * 0.5
        total += (masked(up, keep_up_1) - masked(down, keep_down_1)) * 0.5
        rhs = load_ref[i] - found_ref[i] * ex[E_DISP, 2 + i, inner, :] + total
        put(E_R, i, rhs)
        packed = pack_plane(packed, rhs, i)
        r_[i] = rhs
        p_[i] = rhs
        x_[i] = jnp.zeros((NY, NZ), F32)
        u_[i] = jnp.zeros((NY, NZ), F32)
        if i == OUTSIDE[-1]:
            start(E_R, 2, y=False, z=False)
    zsend[E_R] = packed
    start(E_R, 2, x=False)
    for i in range(NX):
        up, down = shifted_z(ex[E_TAN, 2 + i, inner, :], message_t, i, 1)
        z_up, z_down = masked(up, keep_up_1) * 0.25, masked(down, keep_down_1) * 0.25
        x_up, x_down = ex[E_TAN, 3 + i, inner, :] * 0.25, ex[E_TAN, 1 + i, inner, :] * 0.25
        y_up, y_down = ex[E_TAN, 2 + i, 9 : 9 + NY, :] * 0.25, ex[E_TAN, 2 + i, 7 : 7 + NY, :] * 0.25
        coef[0, i] = found_ref[i] + ((x_up + x_down) + (y_up + y_down) + (z_up + z_down)) - SIGMA
        coef[1, i], coef[2, i] = x_up, x_down
        coef[3, i], coef[4, i] = y_up, y_down
        coef[5, i], coef[6, i] = masked(z_up, keep_up_2), masked(z_down, keep_down_2)

    def step(e, target, write, between=lambda: None):
        box = [zeros]

        def store(i, value):
            put(target, i, value)
            write(i, value)
            box[0] = pack_plane(box[0], value, i)

        finish(e, 2, x=False)
        operator(e, INSIDE, store)
        between()
        finish(e, 2, y=False, z=False)
        operator(e, OUTSIDE, store)
        start(target, 2, y=False, z=False)
        zsend[target] = box[0]
        start(target, 2, x=False)

    def write_w(i, value):
        w_[i] = value
        s_[i] = value

    def write_z(i, value):
        z_[i] = value
        t_[i] = value

    step(E_R, E_W, write_w)
    step(E_W, E_T, write_z)
    sums = None
    for i in range(NX):
        sums = add_dots(sums, r_[i], w_[i], p_[i], s_[i], t_[i])
    red_start(0, 0, row_of(sums))

    def block(k, beta):
        e_t, e_u = E_T + 2 * k, E_T + 2 * k + 1

        def write_u(i, value):
            z2_[i] = value - beta * u_[i]
            u_[i] = value

        step(e_t, e_u, write_u, lambda: red_start(k, 1, red_finish(k, 0)))

        def write_v(i, value):
            v_[i] = value

        finish(e_u, 2, x=False)
        operator(e_u, INSIDE, write_v)
        alpha, beta_1, alpha_1, beta_2 = scalars(red_finish(k, 1))
        box = [zeros]
        sums = None

        def update(i):
            p, s, t, u = p_[i], s_[i], t_[i], u_[i]
            x = x_[i] + alpha * p
            r = r_[i] - alpha * (s + SIGMA * p)
            w = w_[i] - alpha * (t + SIGMA * s)
            z = z_[i] - alpha * (u + SIGMA * t)
            z2 = z2_[i] - alpha * (v_[i] + SIGMA * u)
            p = r + beta_1 * p
            s = w + beta_1 * s
            t = z + beta_1 * t
            u = z2 + beta_1 * u
            x_[i] = x + alpha_1 * p
            r = r - alpha_1 * (s + SIGMA * p)
            w = w - alpha_1 * (t + SIGMA * s)
            z = z - alpha_1 * (u + SIGMA * t)
            r_[i], w_[i], z_[i], u_[i] = r, w, z, u
            p = r + beta_2 * p
            s = w + beta_2 * s
            t = z + beta_2 * t
            p_[i], s_[i], t_[i] = p, s, t
            put(e_t + 2, i, t)
            box[0] = pack_plane(box[0], t, i)

        for i in INSIDE:
            update(i)
            sums = add_dots(sums, r_[i], w_[i], p_[i], s_[i], t_[i])
        finish(e_u, 2, y=False, z=False)
        operator(e_u, OUTSIDE, write_v)
        for i in OUTSIDE:
            update(i)

        @pl.when(k < 2)
        def _():
            start(e_t + 2, 2, y=False, z=False)
            zsend[e_t + 2] = box[0]
            start(e_t + 2, 2, x=False)

        for i in OUTSIDE:
            sums = add_dots(sums, r_[i], w_[i], p_[i], s_[i], t_[i])
        red_start(k + 1, 0, row_of(sums))
        return beta_2

    lax.fori_loop(0, 3, block, jnp.zeros((NY, NZ), F32))

    last = N_RED - 1
    red_start(last, 1, red_finish(last, 0))
    alpha, beta_1, alpha_1, _ = scalars(red_finish(last, 1))
    for i in range(NX):
        p, s, t = p_[i], s_[i], t_[i]
        x = x_[i] + alpha * p
        r = r_[i] - alpha * (s + SIGMA * p)
        w = w_[i] - alpha * (t + SIGMA * s)
        p = r + beta_1 * p
        s = w + beta_1 * s
        change = alpha_1 * (s + SIGMA * p)
        field_out[i] = (ex[E_DISP, 2 + i, inner, :] + (x + alpha_1 * p)) + change
        residual_out[i] = r
        change_out[i] = change

    drain(E_DISP, 1)
    drain(E_SX, 1, y=False)
    drain(E_TAN, 1, y=False)

    def drain_step(e, carry):
        drain(e, 2)
        return carry

    lax.fori_loop(E_R, N_EX, drain_step, 0)

    def drain_red(k, carry):
        red_drain(k)
        return carry

    lax.fori_loop(0, N_RED, drain_red, 0)


def body(displacement, load_field, foundation, flags, slots, family_in, family_mid, family_out, family_tan):
    family_in, family_out = jnp.transpose(family_in, (1, 0, 2)), jnp.transpose(family_out, (1, 0, 2))
    shape = (NX, NY, NZ)
    field = pltpu.VMEM(shape, F32)
    ints = pltpu.VMEM(shape, jnp.int32)
    whole = pl.BlockSpec(memory_space=pltpu.VMEM)
    field_and_change, residual, change = pl.pallas_call(
        newton_kernel,
        out_shape=(jax.ShapeDtypeStruct(shape, F32),) * 3,
        in_specs=[pl.BlockSpec(memory_space=pl.ANY)] * 9,
        out_specs=(whole,) * 3,
        scratch_shapes=[
            field,
            field,
            ints,
            ints,
            pltpu.VMEM((3, FAMILIES, MODES), F32),
            pltpu.VMEM((3, FAMILIES, MODES), BF16),
            pltpu.VMEM((FAMILIES, MODES), F32),
            pltpu.VMEM((N_EX + 1, NX + 4, NY + 16, NZ), F32),
            pltpu.VMEM((N_EX, 8, NZ), F32),
            pltpu.VMEM((N_EX, 8, NZ), F32),
            pltpu.VMEM((N_RED, 2, 16, 1, NZ), F32),
            pltpu.VMEM((FIX + 64, NZ), F32),
            pltpu.VMEM((MODES, 64), BF16),
            pltpu.VMEM((MODES, FAMILIES * MODES), BF16),
            pltpu.VMEM((32, 2 * MODES), BF16),
            pltpu.VMEM((7,) + shape, F32),
            field,
        ]
        + [field] * 10
        + [
            pltpu.SemaphoreType.DMA((N_EX, 5)),
            pltpu.SemaphoreType.DMA((N_EX, 5)),
            pltpu.SemaphoreType.DMA((N_RED, 32)),
            pltpu.SemaphoreType.DMA((N_RED, 32)),
            pltpu.SemaphoreType.DMA((N_IN,)),
        ],
        compiler_params=pltpu.CompilerParams(
            collective_id=0, has_side_effects=True, vmem_limit_bytes=60 * 1024 * 1024
        ),
        name="newton_step",
    )(displacement, load_field, foundation, flags, slots, family_in, family_mid, family_out, family_tan)
    return field_and_change - change, residual - change


def solution(mesh):
    placed = P("blk", "micro", "slab")
    return jax.shard_map(
        body,
        mesh=mesh,
        in_specs=(placed,) * 5 + (P(),) * 4,
        out_specs=(placed, placed),
        check_vma=False,
    )
```

```python
import jax
import jax.numpy as jnp
from jax import lax
from jax.experimental import pallas as pl
from jax.experimental.pallas import tpu as pltpu
from jax.sharding import PartitionSpec as P

F32 = jnp.float32
BF16 = jnp.bfloat16
MESH = pl.DeviceIdType.MESH
FAMILIES = 4
MODES = 256
CAP_SHIFT = 14
SIGMA = 3.0
NX, NY, NZ = 8, 32, 128
TILES = NY // 8
E_DISP, E_TAN, E_SX, E_SY, E_R, E_W, E_T = 0, 1, 2, 3, 4, 5, 6
N_EX = 12
INSIDE = (2, 3, 4, 5)
OUTSIDE = (0, 1, 6, 7)
N_RED = 4
N_IN = 12
FIX = NX * NY * 8
N_DOT = 13


def prepare_weights(family_in, family_out, family_tan, w_in, w_out):
    zero = jnp.zeros((1, MODES), F32)
    high, low, stress, tangent = [], [], [], []
    for f in range(FAMILIES):
        weight = family_in[:, f, :]
        rounded = weight.astype(BF16).astype(F32)
        high += [rounded, rounded, zero, zero]
        low += [weight - rounded, zero, zero, zero, zero, zero]
        tan = family_tan[f : f + 1, :]
        tan_high = tan.astype(BF16).astype(F32)
        stress += [family_out[:, f, :].astype(F32)] + [zero] * 5
        tangent += [zero] * 3 + [tan_high, tan - tan_high] + [zero] * 3
    w_in[...] = jnp.concatenate(high + low, axis=0).T.astype(BF16)
    w_out[:, :MODES] = jnp.concatenate(stress, axis=0).astype(BF16)
    w_out[:, MODES:] = jnp.concatenate(tangent, axis=0).astype(BF16)


def fibre_chunk(points, w_in, w_mid, w_out, places):
    width = len(places) * NZ
    rows = jnp.concatenate([points[pl.ds(place, 8), :] for place in places], axis=1)
    family, flag = rows[6:7, :], rows[7:8, :]
    family_8 = jnp.broadcast_to(family, (8, width))
    chosen = [family_8 == float(f) for f in range(FAMILIES)]
    strain = jnp.concatenate([jnp.where(m, rows, 0.0) for m in chosen], axis=0).astype(BF16)
    modal = jnp.dot(w_in[...], jnp.concatenate([strain, strain], axis=0), preferred_element_type=F32)
    modal = modal.reshape(MODES // 8, 8, width)
    plastic = jnp.broadcast_to(flag, (8, width)) > 0.5
    active = jnp.where(plastic[None], jnp.tanh(modal), modal).reshape(MODES, width).astype(BF16)
    active = active.reshape(MODES // 16, 16, width)
    family_16 = jnp.broadcast_to(family, (16, width))
    parts = []
    for f in range(FAMILIES):
        mask = jnp.where(family_16 == float(f), 1.0, 0.0).astype(BF16)
        parts.append((active * mask[None]).reshape(MODES, width))
    hidden = jnp.dot(w_mid[...], jnp.concatenate(parts, axis=0), preferred_element_type=F32)
    bounded = jnp.tanh(hidden).astype(BF16)
    out = jnp.dot(
        w_out[...], jnp.concatenate([bounded, bounded * bounded], axis=0), preferred_element_type=F32
    )
    picked = jnp.where(
        chosen[0], out[0:8], jnp.where(chosen[1], out[8:16], jnp.where(chosen[2], out[16:24], out[24:32]))
    )
    for i, place in enumerate(places):
        points[pl.ds(place, 8), :] = picked[:, i * NZ : (i + 1) * NZ]


def newton_kernel(
    disp_hbm, load_hbm, found_hbm, flags_hbm, slot_hbm, fin_hbm, fmid_hbm, fout_hbm, ftan_hbm,
    field_out, residual_out, change_out,
    load_ref, found_ref, flags_ref, slot_ref, fin_ref, fout_ref, ftan_ref,
    ex, zsend, zrecv, red, points, w_in, w_mid, w_out, coef, s_z,
    x_, r_, w_, z_, z2_, p_, s_, t_, u_, v_,
    send_sem, recv_sem, red_send, red_recv, in_sem,
):
    inner = pl.ds(8, NY)
    pairs = [(disp_hbm, ex.at[E_DISP, pl.ds(2, NX), inner, :]), (slot_hbm, slot_ref), (flags_hbm, flags_ref)]
    pairs += [(fin_hbm, fin_ref), (fout_hbm, fout_ref), (ftan_hbm, ftan_ref)]
    pairs += [(fmid_hbm.at[f], w_mid.at[:, pl.ds(f * MODES, MODES)]) for f in range(FAMILIES)]
    pairs += [(found_hbm, found_ref), (load_hbm, load_ref)]
    loads = [pltpu.make_async_copy(a, b, in_sem.at[j]) for j, (a, b) in enumerate(pairs)]
    for c in loads:
        c.start()
    blk, slab, micro = lax.axis_index("blk"), lax.axis_index("slab"), lax.axis_index("micro")
    n_blk = lax.axis_size("blk")
    up_blk, down_blk = lax.rem(blk + 1, n_blk), lax.rem(blk + n_blk - 1, n_blk)
    part_x = slab * 4 + micro

    def peer_x(step):
        other = lax.rem(part_x + step, 8)
        return (blk, lax.div(other, 4), lax.rem(other, 4))

    def peer_blk(step):
        return (lax.rem(blk + step, n_blk), slab, micro)

    barrier = pltpu.get_barrier_semaphore()
    friends = [peer_x(j) for j in range(1, 8)] + [peer_blk(j) for j in range(1, 16)]
    for friend in friends:
        pl.semaphore_signal(barrier, inc=1, device_id=friend, device_id_type=MESH)

    lane = lax.broadcasted_iota(jnp.int32, (8, NZ), 1)
    diagonal = lax.broadcasted_iota(jnp.int32, (16, NZ), 0) == lax.broadcasted_iota(jnp.int32, (16, NZ), 1)
    first_slab, last_slab = slab == 0, slab == 1
    pack_id = {n: lax.div(lax.rem(lane + n * (1 - slab), NZ), n) for n in (1, 2)}
    edge_own = jnp.logical_or(jnp.logical_and(lane == NZ - 1, slab == 0), jnp.logical_and(lane == 0, slab == 1))
    edge_up = {n: jnp.logical_and(lane < n, first_slab) for n in (1, 2)}
    edge_down = {n: jnp.logical_and(lane >= NZ - n, last_slab) for n in (1, 2)}

    def keep(condition):
        return jnp.where(condition, 0.0, 1.0).astype(F32)

    keep_up_1 = keep(jnp.logical_and(lane == NZ - 1, last_slab))[None]
    keep_down_1 = keep(jnp.logical_and(lane == 0, first_slab))[None]
    keep_up_2 = keep(jnp.logical_and(lane >= NZ - 2, last_slab))[None]
    keep_down_2 = keep(jnp.logical_and(lane < 2, first_slab))[None]

    @pl.when(micro == 0)
    def _():
        for e in range(N_EX):
            ex[e, :, 0:8, :] = jnp.zeros((NX + 4, 8, NZ), F32)

    @pl.when(micro == 3)
    def _():
        for e in range(N_EX):
            ex[e, :, NY + 8 : NY + 16, :] = jnp.zeros((NX + 4, 8, NZ), F32)

    def copy(source, target, e, k, device):
        return pltpu.make_async_remote_copy(
            src_ref=source, dst_ref=target, send_sem=send_sem.at[e, k], recv_sem=recv_sem.at[e, k],
            device_id=device, device_id_type=MESH,
        )

    def copies_x(e, depth):
        up = copy(
            ex.at[e, pl.ds(NX + 2 - depth, depth), pl.ds(8, NY), :],
            ex.at[e, pl.ds(2 - depth, depth), pl.ds(8, NY), :], e, 0, (up_blk, slab, micro),
        )
        down = copy(
            ex.at[e, pl.ds(2, depth), pl.ds(8, NY), :],
            ex.at[e, pl.ds(NX + 2, depth), pl.ds(8, NY), :], e, 1, (down_blk, slab, micro),
        )
        return up, down

    def copies_y(e):
        up = copy(
            ex.at[e, pl.ds(2, NX), pl.ds(NY, 8), :], ex.at[e, pl.ds(2, NX), pl.ds(0, 8), :],
            e, 2, (blk, slab, lax.rem(micro + 1, 4)),
        )
        down = copy(
            ex.at[e, pl.ds(2, NX), pl.ds(8, 8), :], ex.at[e, pl.ds(2, NX), pl.ds(NY + 8, 8), :],
            e, 3, (blk, slab, lax.rem(micro + 3, 4)),
        )
        return up, down

    def copy_z(e):
        return copy(zsend.at[e], zrecv.at[e], e, 4, (blk, 1 - slab, micro))

    def start(e, depth, x=True, y=True, z=True):
        if x:
            for c in copies_x(e, depth):
                c.start()
        if z:
            copy_z(e).start()
        if y:
            up, down = copies_y(e)

            @pl.when(micro < 3)
            def _():
                up.start()

            @pl.when(micro > 0)
            def _():
                down.start()

    def finish(e, depth, x=True, y=True, z=True):
        if x:
            for c in copies_x(e, depth):
                c.wait_recv()
        if z:
            copy_z(e).wait_recv()
        if y:
            up, down = copies_y(e)

            @pl.when(micro > 0)
            def _():
                up.wait_recv()

            @pl.when(micro < 3)
            def _():
                down.wait_recv()

    def drain(e, depth, x=True, y=True, z=True):
        if x:
            for c in copies_x(e, depth):
                c.wait_send()
        if z:
            copy_z(e).wait_send()
        if y:
            up, down = copies_y(e)

            @pl.when(micro < 3)
            def _():
                up.wait_send()

            @pl.when(micro > 0)
            def _():
                down.wait_send()

    def pack_plane(packed, plane, i, step=2):
        for q in range(TILES):
            n = i * TILES + q
            tile = plane[8 * q : 8 * q + 8]
            packed = jnp.where(pack_id[step] == n, pltpu.roll(tile, step * n, 1) if n else tile, packed)
        return packed

    def shifted_z(plane, message, i, step):
        tiles_up, tiles_down = [], []
        for q in range(TILES):
            n = i * TILES + q
            tile = plane[8 * q : 8 * q + 8]
            halo = pltpu.roll(message, NZ - step * n, 1) if n else message
            tiles_up.append(pltpu.roll(jnp.where(edge_up[step], halo, tile), NZ - step, 1))
            tiles_down.append(pltpu.roll(jnp.where(edge_down[step], halo, tile), step, 1))
        return jnp.concatenate(tiles_up, axis=0), jnp.concatenate(tiles_down, axis=0)

    def masked(plane, mask):
        return (plane.reshape(-1, 8, NZ) * mask).reshape(plane.shape)

    def put(e, i, plane):
        ex[e, 2 + i, inner, :] = plane

    def operator(e, planes, write):
        message = zrecv[e]
        for i in planes:
            value = ex[e, 2 + i, inner, :]
            z_up, z_down = shifted_z(value, message, i, 2)
            total = coef[0, i] * value
            total -= coef[1, i] * ex[e, 4 + i, inner, :] + coef[2, i] * ex[e, i, inner, :]
            total -= coef[3, i] * ex[e, 2 + i, 10 : 10 + NY, :] + coef[4, i] * ex[e, 2 + i, 6 : 6 + NY, :]
            total -= coef[5, i] * z_up + coef[6, i] * z_down
            write(i, total)

    def red_copy(k, stage, step, peer, mine):
        n = stage * 16 + step
        return pltpu.make_async_remote_copy(
            src_ref=red.at[k, stage, mine], dst_ref=red.at[k, stage, mine],
            send_sem=red_send.at[k, n], recv_sem=red_recv.at[k, n], device_id=peer, device_id_type=MESH,
        )

    stages = ((peer_x, part_x, 8), (peer_blk, blk, 16))

    def red_start(k, stage, rows):
        peer, mine, count = stages[stage]
        red[k, stage, mine] = rows
        for step in range(1, count):
            red_copy(k, stage, step, peer(step), mine).start()

    def red_finish(k, stage):
        peer, mine, count = stages[stage]
        for step in range(1, count):
            red_copy(k, stage, step, peer(step), mine).wait_recv()
        total = red[k, stage, 0]
        for j in range(1, count):
            total = total + red[k, stage, j]
        return total

    def red_drain(k):
        for stage, (peer, mine, count) in enumerate(stages):
            for step in range(1, count):
                red_copy(k, stage, step, peer(step), mine).wait_send()

    def add_dots(sums, r, w, p, s, t):
        kp = s + SIGMA * p
        kr = w + SIGMA * r
        kkp = (t + SIGMA * s) + SIGMA * kp
        terms = (
            r * r, r * kp, r * kr, r * kkp, kp * kp, kp * kr, kp * kkp,
            kr * kr, kr * kkp, kkp * kkp, p * kp, p * kr, p * kkp,
        )
        folded = [term.reshape(TILES, 8, NZ).sum(axis=0) for term in terms]
        return folded if sums is None else [a + b for a, b in zip(sums, folded)]

    def row_of(sums):
        rows = [jnp.sum(a, axis=0, keepdims=True) for a in sums]
        rows = jnp.concatenate(rows + [jnp.zeros((16 - N_DOT, NZ), F32)], axis=0)
        sums = jnp.broadcast_to(jnp.sum(rows, axis=1, keepdims=True), (16, NZ))
        return jnp.sum(jnp.where(diagonal, sums, 0.0), axis=0, keepdims=True)

    def scalars(rows):
        d = jnp.sum(jnp.where(diagonal, jnp.broadcast_to(rows, (16, NZ)), 0.0), axis=1, keepdims=True)
        g = [d[j : j + 1, :] for j in range(N_DOT)]
        rr, rs, rw, rt, ss, sw, st, ww, wt, tt, ps, pw, pt = g
        alpha = rr / ps
        rr_1 = rr - 2.0 * alpha * rs + alpha * alpha * ss
        beta_1 = rr_1 / rr
        r_q = rw - alpha * rt + beta_1 * rs
        s_q = sw - alpha * st + beta_1 * ss
        p_q = pw - alpha * pt + beta_1 * ps
        alpha_1 = rr_1 / (r_q - alpha * s_q + beta_1 * p_q)
        w_q = ww - alpha * wt + beta_1 * sw
        t_q = wt - alpha * tt + beta_1 * st
        q_q = w_q - alpha * t_q + beta_1 * s_q
        rr_2 = rr_1 - 2.0 * alpha_1 * (r_q - alpha * s_q) + alpha_1 * alpha_1 * q_q
        beta_2 = rr_2 / rr_1
        return [jnp.broadcast_to(a, (NY, NZ)) for a in (alpha, beta_1, alpha_1, beta_2)]

    zeros = jnp.zeros((8, NZ), F32)

    def strains_at(i, halo):
        value = ex[E_DISP, 2 + i, inner, :]
        if halo is None:
            y_up, y_down = pltpu.roll(value, NY - 1, 0), pltpu.roll(value, 1, 0)
            z_up, z_down = pltpu.roll(value, NZ - 1, 1), pltpu.roll(value, 1, 1)
        else:
            y_up, y_down = ex[E_DISP, 2 + i, 9 : 9 + NY, :], ex[E_DISP, 2 + i, 7 : 7 + NY, :]
            z_up, z_down = shifted_z(value, halo, i, 1)
        return (
            (ex[E_DISP, 3 + i, inner, :] - ex[E_DISP, 1 + i, inner, :]) * 0.5,
            (y_up - y_down) * 0.5,
            (masked(z_up, keep_up_1) - masked(z_down, keep_down_1)) * 0.5,
        )

    def store_points(base, count, strains, family, flag):
        rounded = [s.astype(BF16).astype(F32) for s in strains]
        rows = rounded + [s - h for s, h in zip(strains, rounded)] + [family, flag]
        for k, row in enumerate(rows):
            points[pl.ds(base + k, count, stride=8), :] = row

    def traits(i):
        family = lax.shift_right_logical(slot_ref[i], CAP_SHIFT).astype(F32)
        return family, flags_ref[i].astype(F32)

    def chunks(first, last, size, start_of):
        def chunk(j, carry):
            fibre_chunk(points, w_in, w_mid, w_out, [start_of(j * size + i) for i in range(size)])
            return carry

        lax.fori_loop(first, last, chunk, 0)

    def inner_row(m):
        n = lax.div(m, NY - 2)
        plane = n + 1 + 2 * lax.div(n, 2) - 6 * lax.div(n, 4)
        return pl.multiple_of((plane * NY + lax.rem(m, NY - 2) + 1) * 8, 8)

    def face_row(m):
        return pl.multiple_of((m + lax.div(m, NY) * ((NX - 2) * NY)) * 8, 8)

    middle = range(1, NX - 1)
    loads[0].wait()
    packed = zeros
    for i in range(NX):
        packed = pack_plane(packed, ex[E_DISP, 2 + i, inner, :], i, 1)
    zsend[E_DISP] = packed
    loads[1].wait()
    loads[2].wait()
    for i in middle:
        store_points(i * NY * 8, NY, strains_at(i, None), *traits(i))
    for c in loads[3:10]:
        c.wait()
    prepare_weights(fin_ref, fout_ref, ftan_ref, w_in, w_out)

    chunks(0, 1, 32, inner_row)
    pl.semaphore_wait(barrier, len(friends))
    start(E_DISP, 1)
    chunks(1, 3, 32, inner_row)
    finish(E_DISP, 1)
    message = zrecv[E_DISP]
    edges = [zeros] * 5
    for i in range(NX):
        columns = strains_at(i, message) + traits(i)
        edges = [pack_plane(e, c, i, 1) for e, c in zip(edges, columns)]
        if i in middle:
            for y in (0, NY - 1):
                part = [c[y : y + 1] for c in columns]
                store_points((i * NY + y) * 8, 1, part[:3], part[3], part[4])
        else:
            store_points(i * NY * 8, NY, columns[:3], columns[3], columns[4])
    store_points(FIX, 8, edges[:3], edges[3], edges[4])
    sides = [(i * NY + y) * 8 for i in middle for y in (0, NY - 1)]
    rest = [(4 * NY + y) * 8 for y in range(NY - 5, NY - 1)]
    fibre_chunk(points, w_in, w_mid, w_out, [FIX + 8 * i for i in range(8)] + sides + rest)
    chunks(0, 2, 32, face_row)

    def results(base, count):
        sx, sy, sz, high, low = [points[pl.ds(base + k, count, stride=8), :] for k in range(5)]
        return sx, sy, sz, 0.5 + (high + low)

    def keep_results(i, top, count, values):
        rows = pl.ds(8 + top, count)
        ex[E_SX, 2 + i, rows, :] = values[0]
        ex[E_SY, 2 + i, rows, :] = values[1]
        s_z[i, pl.ds(top, count), :] = values[2]
        ex[E_TAN, 2 + i, rows, :] = values[3]

    edges = results(FIX, 8)
    zsend[E_SX] = edges[2]
    zsend[E_TAN] = edges[3]
    for i in range(NX):
        if i in middle:
            for y in (0, NY - 1):
                keep_results(i, y, 1, results((i * NY + y) * 8, 1))
        else:
            keep_results(i, 0, NY, results(i * NY * 8, NY))
    start(E_SX, 1, y=False)
    start(E_TAN, 1)
    start(E_SY, 1, x=False, z=False)
    chunks(0, 1, 40, lambda m: inner_row(m + 96))
    drain(E_TAN, 1, x=False, z=False)
    drain(E_SY, 1, x=False, z=False)
    def take_plane(i):
        values = results(i * NY * 8, NY)
        columns = []
        for e, v in zip(edges, values):
            tiles = [
                jnp.where(edge_own, pltpu.roll(e, NZ - (i * TILES + q), 1), v[8 * q : 8 * q + 8])
                for q in range(TILES)
            ]
            columns.append(jnp.concatenate(tiles, axis=0))
        keep_results(i, 0, NY, columns)

    for i in (1, 2, 5, 6):
        take_plane(i)

    loads[10].wait()
    loads[11].wait()
    finish(E_SX, 1, y=False)
    finish(E_TAN, 1)
    finish(E_SY, 1, x=False, z=False)
    message_s, message_t = zrecv[E_SX], zrecv[E_TAN]
    packed = zeros
    for i in OUTSIDE + INSIDE:
        if i == INSIDE[0]:
            chunks(0, 1, 40, lambda m: inner_row(m + 136))
            take_plane(3)
            take_plane(4)
        up, down = shifted_z(s_z[i], message_s, i, 1)
        total = (ex[E_SX, 3 + i, inner, :] - ex[E_SX, 1 + i, inner, :]) * 0.5
        total += (ex[E_SY, 2 + i, 9 : 9 + NY, :] - ex[E_SY, 2 + i, 7 : 7 + NY, :]) * 0.5
        total += (masked(up, keep_up_1) - masked(down, keep_down_1)) * 0.5
        rhs = load_ref[i] - found_ref[i] * ex[E_DISP, 2 + i, inner, :] + total
        put(E_R, i, rhs)
        packed = pack_plane(packed, rhs, i)
        r_[i] = rhs
        p_[i] = rhs
        x_[i] = jnp.zeros((NY, NZ), F32)
        u_[i] = jnp.zeros((NY, NZ), F32)
        if i == OUTSIDE[-1]:
            start(E_R, 2, y=False, z=False)
    zsend[E_R] = packed
    start(E_R, 2, x=False)
    for i in range(NX):
        up, down = shifted_z(ex[E_TAN, 2 + i, inner, :], message_t, i, 1)
        z_up, z_down = masked(up, keep_up_1) * 0.25, masked(down, keep_down_1) * 0.25
        x_up, x_down = ex[E_TAN, 3 + i, inner, :] * 0.25, ex[E_TAN, 1 + i, inner, :] * 0.25
        y_up, y_down = ex[E_TAN, 2 + i, 9 : 9 + NY, :] * 0.25, ex[E_TAN, 2 + i, 7 : 7 + NY, :] * 0.25
        coef[0, i] = found_ref[i] + ((x_up + x_down) + (y_up + y_down) + (z_up + z_down)) - SIGMA
        coef[1, i], coef[2, i] = x_up, x_down
        coef[3, i], coef[4, i] = y_up, y_down
        coef[5, i], coef[6, i] = masked(z_up, keep_up_2), masked(z_down, keep_down_2)

    def step(e, target, write, between=lambda: None):
        box = [zeros]

        def store(i, value):
            put(target, i, value)
            write(i, value)
            box[0] = pack_plane(box[0], value, i)

        finish(e, 2, x=False)
        operator(e, INSIDE, store)
        between()
        finish(e, 2, y=False, z=False)
        operator(e, OUTSIDE, store)
        start(target, 2, y=False, z=False)
        zsend[target] = box[0]
        start(target, 2, x=False)

    def write_w(i, value):
        w_[i] = value
        s_[i] = value

    def write_z(i, value):
        z_[i] = value
        t_[i] = value

    step(E_R, E_W, write_w)
    step(E_W, E_T, write_z)
    sums = None
    for i in range(NX):
        sums = add_dots(sums, r_[i], w_[i], p_[i], s_[i], t_[i])
    red_start(0, 0, row_of(sums))

    def block(k, beta):
        e_t, e_u = E_T + 2 * k, E_T + 2 * k + 1

        def write_u(i, value):
            z2_[i] = value - beta * u_[i]
            u_[i] = value

        step(e_t, e_u, write_u, lambda: red_start(k, 1, red_finish(k, 0)))

        def write_v(i, value):
            v_[i] = value

        finish(e_u, 2, x=False)
        operator(e_u, INSIDE, write_v)
        alpha, beta_1, alpha_1, beta_2 = scalars(red_finish(k, 1))
        box = [zeros]
        sums = None

        def update(i):
            p, s, t, u = p_[i], s_[i], t_[i], u_[i]
            x = x_[i] + alpha * p
            r = r_[i] - alpha * (s + SIGMA * p)
            w = w_[i] - alpha * (t + SIGMA * s)
            z = z_[i] - alpha * (u + SIGMA * t)
            z2 = z2_[i] - alpha * (v_[i] + SIGMA * u)
            p = r + beta_1 * p
            s = w + beta_1 * s
            t = z + beta_1 * t
            u = z2 + beta_1 * u
            x_[i] = x + alpha_1 * p
            r = r - alpha_1 * (s + SIGMA * p)
            w = w - alpha_1 * (t + SIGMA * s)
            z = z - alpha_1 * (u + SIGMA * t)
            r_[i], w_[i], z_[i], u_[i] = r, w, z, u
            p = r + beta_2 * p
            s = w + beta_2 * s
            t = z + beta_2 * t
            p_[i], s_[i], t_[i] = p, s, t
            put(e_t + 2, i, t)
            box[0] = pack_plane(box[0], t, i)

        for i in INSIDE:
            update(i)
            sums = add_dots(sums, r_[i], w_[i], p_[i], s_[i], t_[i])
        finish(e_u, 2, y=False, z=False)
        operator(e_u, OUTSIDE, write_v)
        for i in OUTSIDE:
            update(i)

        @pl.when(k < 2)
        def _():
            start(e_t + 2, 2, y=False, z=False)
            zsend[e_t + 2] = box[0]
            start(e_t + 2, 2, x=False)

        for i in OUTSIDE:
            sums = add_dots(sums, r_[i], w_[i], p_[i], s_[i], t_[i])
        red_start(k + 1, 0, row_of(sums))
        return beta_2

    lax.fori_loop(0, 3, block, jnp.zeros((NY, NZ), F32))

    last = N_RED - 1
    red_start(last, 1, red_finish(last, 0))
    alpha, beta_1, alpha_1, _ = scalars(red_finish(last, 1))
    for i in range(NX):
        p, s, t = p_[i], s_[i], t_[i]
        x = x_[i] + alpha * p
        r = r_[i] - alpha * (s + SIGMA * p)
        w = w_[i] - alpha * (t + SIGMA * s)
        p = r + beta_1 * p
        s = w + beta_1 * s
        change = alpha_1 * (s + SIGMA * p)
        field_out[i] = (ex[E_DISP, 2 + i, inner, :] + (x + alpha_1 * p)) + change
        residual_out[i] = r
        change_out[i] = change

    drain(E_DISP, 1)
    drain(E_SX, 1, y=False)
    drain(E_TAN, 1, y=False)

    def drain_step(e, carry):
        drain(e, 2)
        return carry

    lax.fori_loop(E_R, N_EX, drain_step, 0)

    def drain_red(k, carry):
        red_drain(k)
        return carry

    lax.fori_loop(0, N_RED, drain_red, 0)


def body(displacement, load_field, foundation, flags, slots, family_in, family_mid, family_out, family_tan):
    family_in, family_out = jnp.transpose(family_in, (1, 0, 2)), jnp.transpose(family_out, (1, 0, 2))
    shape = (NX, NY, NZ)
    field = pltpu.VMEM(shape, F32)
    ints = pltpu.VMEM(shape, jnp.int32)
    whole = pl.BlockSpec(memory_space=pltpu.VMEM)
    field_and_change, residual, change = pl.pallas_call(
        newton_kernel,
        out_shape=(jax.ShapeDtypeStruct(shape, F32),) * 3,
        in_specs=[pl.BlockSpec(memory_space=pl.ANY)] * 9,
        out_specs=(whole,) * 3,
        scratch_shapes=[
            field,
            field,
            ints,
            ints,
            pltpu.VMEM((3, FAMILIES, MODES), F32),
            pltpu.VMEM((3, FAMILIES, MODES), BF16),
            pltpu.VMEM((FAMILIES, MODES), F32),
            pltpu.VMEM((N_EX + 1, NX + 4, NY + 16, NZ), F32),
            pltpu.VMEM((N_EX, 8, NZ), F32),
            pltpu.VMEM((N_EX, 8, NZ), F32),
            pltpu.VMEM((N_RED, 2, 16, 1, NZ), F32),
            pltpu.VMEM((FIX + 64, NZ), F32),
            pltpu.VMEM((MODES, 64), BF16),
            pltpu.VMEM((MODES, FAMILIES * MODES), BF16),
            pltpu.VMEM((32, 2 * MODES), BF16),
            pltpu.VMEM((7,) + shape, F32),
            field,
        ]
        + [field] * 10
        + [
            pltpu.SemaphoreType.DMA((N_EX, 5)),
            pltpu.SemaphoreType.DMA((N_EX, 5)),
            pltpu.SemaphoreType.DMA((N_RED, 32)),
            pltpu.SemaphoreType.DMA((N_RED, 32)),
            pltpu.SemaphoreType.DMA((N_IN,)),
        ],
        compiler_params=pltpu.CompilerParams(
            collective_id=0, has_side_effects=True, vmem_limit_bytes=60 * 1024 * 1024
        ),
        name="newton_step",
    )(displacement, load_field, foundation, flags, slots, family_in, family_mid, family_out, family_tan)
    return field_and_change - change, residual - change


def solution(mesh):
    placed = P("blk", "micro", "slab")
    return jax.shard_map(
        body,
        mesh=mesh,
        in_specs=(placed,) * 5 + (P(),) * 4,
        out_specs=(placed, placed),
        check_vma=False,
    )
```
